512 devices in a mesh: seq: 128 (over z, y_lo, x), ch: 4 (over y_hi, core).
Axes of the slice: x: 4, y: 8 (y_hi: 2, y_lo: 4; y = y_hi * 4 + y_lo), z: 8, core: 2. Of those that a mesh axis runs over, the one named last changes fastest.
Arguments:
- inputs: float32 [768, 32768], P('ch', 'seq'), may hold values from -24 to 24
- weight: bfloat16 [3, 768, 768], P(None, 'ch'), may hold values from -0.125 to 0.125
- grad_out: float32 [768, 32768], P('ch', 'seq'), may hold values from -6 to 6
Outputs:
- outputs: float32 [768, 32768], P('ch', 'seq')
- grad_inputs: float32 [768, 32768], P('ch', 'seq')
- grad_weight: float32 [3, 768, 768], P(None, 'seq', 'ch')
The draws below stay inside these ranges and needn't reach their ends.
All inputs are finite; a program needn't handle non-finite values.
Results may differ from the reference program's by a relative error of at most 0.0047.
Values may be sent and summed in bfloat16 or wider, within the bound.
A program may use at most 64 MiB of HBM per device.

```python
import math
import jax
import jax.numpy as jnp

C = 768
TOKENS = 32768
DILATION = 2048
N_CH = 4


def raised(values, stream_key, source, target, parts, factor):
    owner, partner = [(jnp.arange(values.shape[dim]) // (values.shape[dim] // parts)).reshape([-1 if axis == dim else 1 for axis in range(values.ndim)]) for dim in (source, target)]
    chosen = jax.random.permutation(stream_key, parts)[partner]
    strong = (owner == chosen) | (owner == (partner + parts // 2) % parts)
    return jnp.where(strong, factor * values, values)


def steps_of(stream_key, dims, split, low, top_value):
    loudness, own = 1.0, jax.random.fold_in(stream_key, 6)
    for dim, blocks in split:
        draws = jnp.exp(jax.random.uniform(jax.random.fold_in(own, dim), (blocks,), jnp.float32, low / len(split), top_value / len(split)))
        loudness = loudness * jnp.repeat(draws, dims[dim] // blocks).reshape([-1 if axis == dim else 1 for axis in range(len(dims))])
    return loudness


def bell_draw(own_key, shape, scale, limit, shards=(), kind=jnp.bfloat16):
    drawn = scale * jax.random.normal(own_key, shape, jnp.float32)
    if shards:
        drawn = drawn * steps_of(own_key, shape, shards, -0.22, 0.18)
    return jnp.clip(drawn, -limit, limit).astype(kind)


def heavy_noise(rng, shape, spread, most, shards, heavy, held_as=jnp.bfloat16):
    values = spread * jax.random.normal(rng, shape, jnp.float32)
    if shards:
        values = values * steps_of(rng, shape, shards, -0.22, 0.18)
    return jnp.clip(raised(values, jax.random.fold_in(rng, 3), *heavy), -most, most).astype(held_as)


def setup_inputs(seed: int = 0) -> dict:
    splits = jax.random.split(jax.random.key(seed), 4)
    inputs = heavy_noise(splits[0], (C, TOKENS), 1.0, 24.0, ((0, 4), (1, 128)), (1, 0, 128, 5.5), jnp.float32)
    weight = bell_draw(splits[1], (3, C, C), (3 * C) ** -0.5, 0.125, ((1, 4),))
    grad_out = bell_draw(splits[2], (C, TOKENS), 1.0, 6.0, ((0, 4), (1, 128)), jnp.float32)
    return dict(inputs=inputs, weight=weight, grad_out=grad_out)


def gelu_parts(value):
    cdf = 0.5 * (1.0 + jax.scipy.special.erf(value * (1.0 / math.sqrt(2.0))))
    pdf = jnp.exp(-0.5 * value * value) * (1.0 / math.sqrt(2.0 * math.pi))
    return (value * cdf, cdf + value * pdf)

def shifted(block, offset):
    zeros = jnp.zeros((block.shape[0], DILATION), block.dtype)
    if offset > 0:
        return jnp.concatenate([zeros, block[:, :-DILATION]], axis=1)
    return jnp.concatenate([block[:, DILATION:], zeros], axis=1)

def reference(inputs, weight, grad_out):
    lowered = inputs.astype(jnp.bfloat16)
    before = shifted(lowered, 1)
    after = shifted(lowered, -1)
    preact = jnp.dot(weight[0], before, preferred_element_type=jnp.float32)
    preact = preact + jnp.dot(weight[1], lowered, preferred_element_type=jnp.float32)
    preact = preact + jnp.dot(weight[2], after, preferred_element_type=jnp.float32)
    act, deriv = gelu_parts(preact)
    outputs = inputs + act
    delta = (grad_out * deriv).astype(jnp.bfloat16)
    delta_after = shifted(delta, -1)
    delta_before = shifted(delta, 1)
    group = C // N_CH
    total = jnp.zeros(inputs.shape, jnp.float32)
    for index in range(N_CH):
        low = index * group
        high = low + group
        part = jnp.dot(weight[0][low:high].T, delta_after[low:high], preferred_element_type=jnp.float32)
        part = part + jnp.dot(weight[1][low:high].T, delta[low:high], preferred_element_type=jnp.float32)
        part = part + jnp.dot(weight[2][low:high].T, delta_before[low:high], preferred_element_type=jnp.float32)
        total = total + part.astype(jnp.bfloat16).astype(jnp.float32)
    grad_inputs = grad_out + total
    scale = TOKENS ** (-0.5)
    grad_weight = jnp.stack([jnp.dot(before, delta.T, preferred_element_type=jnp.float32), jnp.dot(lowered, delta.T, preferred_element_type=jnp.float32), jnp.dot(after, delta.T, preferred_element_type=jnp.float32)]) * scale
    return (outputs, grad_inputs, grad_weight)
```

```python
import math

import jax
import jax.numpy as jnp
from jax import lax
from jax.experimental import pallas as pl
from jax.experimental.pallas import tpu as pltpu
from jax.sharding import PartitionSpec as P

MESH = pl.DeviceIdType.MESH
F32, BF16 = jnp.float32, jnp.bfloat16
GROUP = 192
HALF = GROUP // 2
COLS = 256
LANES = 640

NAMES = []
for k in range(2):
    NAMES += [f"{n}{k}" for n in ("own", "up", "dn", "zu", "zd", "cup", "cdn", "czu", "czd", "cr", "dy", "dz")]
NAMES += ["rup", "rdn", "rs0", "rs1", "fa", "fb", "ga", "gb"]
NAMES += ["x1a", "x1b", "x2a", "x2b", "x2c", "x2d"]
NAMES += [f"y{d}" for d in range(1, 4)] + [f"z{d}" for d in range(1, 8)]
SLOT = {name: i for i, name in enumerate(NAMES)}


def dot(a, b, ca, cb):
    return lax.dot_general(a, b, (((ca,), (cb,)), ((), ())), preferred_element_type=F32)


def one_hot(hit):
    return jnp.where(hit, 1.0, 0.0).astype(BF16)


def kernel(
    scale, x_ref, w_ref, g_ref, out_ref, gin_ref, gw_ref,
    xb, wp, db, ds, ps, pown, xr1, xs2, xr2, ys, yr, zs, zr, rf, rb, rs1r, rs2s, rel, rs2r, send, recv,
):
    s, ch = lax.axis_index("seq"), lax.axis_index("ch")
    z, yl, x = lax.div(s, 16), lax.rem(lax.div(s, 4), 4), lax.rem(s, 4)
    yh, c = lax.div(ch, 2), lax.rem(ch, 2)
    y = yh * 4 + yl
    late = lax.div(yl, 2)

    def at(z, y, x, c):
        z, y, x = lax.rem(z, 8), lax.rem(y, 8), lax.rem(x, 4)
        return (z * 16 + lax.rem(y, 4) * 4 + x, lax.div(y, 4) * 2 + c)

    def ch_of(y):
        return lax.div(lax.rem(y, 8), 4) * 2 + c

    core = at(z, y, x, 1 - c)
    y_up, y_dn = at(z, y + 2, x, c), at(z, y + 6, x, c)
    x_up, x_dn = at(z, y, x + 1, c), at(z, y, x + 3, c)
    y_in = at(z, yh * 4 + lax.rem(yl + 2, 4), x, c)
    z_to = at(z + 1 + 6 * late, y, x, c)
    y_of = [None] + [at(z, yh * 4 + lax.rem(yl + d, 4), x, c) for d in range(1, 4)]
    z_of = [None] + [at(z + d, y, x, c) for d in range(1, 8)]

    barrier = pltpu.get_barrier_semaphore()
    peers = [core, y_up, y_dn, x_up, x_dn] + y_of[1:] + z_of[1:]
    for peer in peers:
        pl.semaphore_signal(barrier, inc=1, device_id=peer, device_id_type=MESH)

    live = {}

    def go(name, src, dst, to):
        i = SLOT[name]
        live[name] = pltpu.make_async_remote_copy(
            src_ref=src, dst_ref=dst, send_sem=send.at[i], recv_sem=recv.at[i], device_id=to, device_id_type=MESH
        )
        live[name].start()

    def got(name):
        live[name].wait_recv()

    row = lax.broadcasted_iota(jnp.int32, (384, 384), 0)
    col = lax.broadcasted_iota(jnp.int32, (384, 384), 1)
    upper = jnp.where(row >= GROUP, 1, 0)
    r = row - GROUP * upper
    six = lax.shift_right_logical(r * 10923, 16)
    source = (six & 1) * 96 + (lax.shift_right_logical(six, 1) & 3) * 24 + lax.shift_right_logical(six, 3) * 6 + r - six * 6
    order = one_hot(source + GROUP * upper == col)
    lowered = x_ref[...].astype(BF16)
    xb[1, ch] = dot(order[:GROUP, :GROUP], lowered, 1, 0).astype(BF16)

    pl.semaphore_wait(barrier, len(peers))

    t_to = 2 * late
    t_in = 2 - 2 * late
    part = [pl.ds(HALF * k, HALF) for k in range(2)]
    ch_dn, ch_up, ch_far = ch_of(y + 6), ch_of(y + 2), ch_of(y + 4)
    for k in range(2):
        mine = xb.at[1, ch, part[k]]
        go(f"up{k}", mine, xb.at[t_to, ch, part[k]], y_up)
        go(f"dn{k}", mine, xb.at[t_to, ch, part[k]], y_dn)
        go(f"own{k}", mine, mine, core)

    for t in range(3):
        for b in range(2):
            cols = slice(384 * b, 384 * (b + 1))
            wp[t, :, cols] = dot(w_ref[t, :, cols], order, 1, 1).astype(BF16)

    for k in range(2):
        got(f"up{k}")
        block = xb.at[t_in, ch_dn, part[k]]
        if k == 0:
            go("rup", block, xb.at[1, ch_dn, part[k]], y_up)
        go(f"zu{k}", block, xb.at[t_to, ch_dn, part[k]], z_to)
        go(f"cup{k}", block, block, core)
        got(f"dn{k}")
        block = xb.at[t_in, ch_up, part[k]]
        if k == 1:
            go("rdn", block, xb.at[1, ch_up, part[k]], y_dn)
        go(f"zd{k}", block, xb.at[t_to, ch_up, part[k]], z_to)
        go(f"cdn{k}", block, block, core)
    for k in range(2):
        got(f"zu{k}")
        block = xb.at[t_to, ch_dn, part[k]]
        go(f"czu{k}", block, block, core)
        got(f"zd{k}")
        block = xb.at[t_to, ch_up, part[k]]
        go(f"czd{k}", block, block, core)
    for k in range(2):
        got(("rup", "rdn")[k])
        block = xb.at[1, ch_far, part[k]]
        go(f"cr{k}", block, block, core)
    for k in range(2):
        for name in ("own", "cup", "cdn", "czu", "czd", "cr"):
            got(f"{name}{k}")

    first = jnp.where(s < 8, 0.0, 1.0).astype(F32)
    last = jnp.where(s >= 120, 0.0, 1.0).astype(F32)
    preact = dot(wp[1], xb[1].reshape(768, COLS), 1, 0)
    preact += dot(wp[0], xb[0].reshape(768, COLS), 1, 0) * first
    preact += dot(wp[2], xb[2].reshape(768, COLS), 1, 0) * last
    cdf = 0.5 * (1.0 + lax.erf(preact * (1.0 / math.sqrt(2.0))))
    pdf = jnp.exp(-0.5 * preact * preact) * (1.0 / math.sqrt(2.0 * math.pi))
    delta32 = g_ref[...] * (cdf + preact * pdf)
    delta = delta32.astype(BF16)
    db[1] = delta

    for k in range(2):
        go(f"dy{k}", db.at[1, part[k]], db.at[t_to, part[k]], y_in)
    out_ref[...] = x_ref[...] + preact * cdf

    zero = jnp.zeros((64, COLS), BF16)
    ds[0:192] = (delta32 * first).astype(BF16)
    ds[192:256] = zero
    ds[256:320] = zero
    ds[320:384] = zero
    ds[384:448] = zero
    ds[448:640] = delta
    ds[640:832] = (delta32 * last).astype(BF16)
    ds[832:896] = zero

    def chunk(step):
        rows = pl.ds(pl.multiple_of(lax.rem(x + step, 4) * 48, 48), 48)
        before, here, after = [xb[t, :, rows, :].reshape(GROUP, COLS) for t in range(3)]
        left = dot(before, ds[0:256], 1, 1) + dot(here, ds[256:512], 1, 1)
        return left, dot(here, ds[512:640], 1, 1), dot(after, ds[640:896], 1, 1)

    def keep(ref, parts, kind):
        ref[:, 0:256] = parts[0].astype(kind)
        ref[:, 256:384] = parts[1].astype(kind)
        ref[:, 384:640] = parts[2].astype(kind)

    keep(ps.at[2], chunk(2), BF16)
    go("x1a", ps.at[2, part[0]], xr1.at[0], x_up)
    go("x1b", ps.at[2, part[1]], xr1.at[1], x_dn)
    keep(ps.at[1], chunk(1), BF16)
    go("x2b", ps.at[1, part[1]], xr2.at[1], x_up)
    keep(ps.at[3], chunk(3), BF16)
    go("x2c", ps.at[3, part[0]], xr2.at[2], x_dn)
    keep(pown, chunk(0), F32)

    for k in range(2):
        got(f"dy{k}")
        go(f"dz{k}", db.at[t_in, part[k]], db.at[t_to, part[k]], z_to)

    got("x1a")
    xs2[0] = (xr1[0].astype(F32) + ps[1, 0:HALF].astype(F32)).astype(BF16)
    go("x2a", xs2.at[0], xr2.at[0], x_up)
    got("x1b")
    xs2[1] = (xr1[1].astype(F32) + ps[3, HALF:GROUP].astype(F32)).astype(BF16)
    go("x2d", xs2.at[1], xr2.at[3], x_dn)

    for k in range(2):
        got(f"dz{k}")
    for q in range(4):
        cols = slice(GROUP * q, GROUP * (q + 1))
        back = dot(w_ref[1, :, cols], db[1], 0, 0)
        back += dot(w_ref[0, :, cols], db[2], 0, 0) * last
        back += dot(w_ref[2, :, cols], db[0], 0, 0) * first
        rf[q] = back
        rb[q] = back.astype(BF16)
    for h in range(2):
        go(f"rs{h}", rb.at[h * 2 + 1 - c], rs1r.at[h], core)
    for h in range(2):
        got(f"rs{h}")
    rs2s[...] = (rf[(1 - yh) * 2 + c] + rs1r[1 - yh].astype(F32)).astype(BF16)
    go("fa", rs2s.at[part[0]], rel.at[0], y_up)
    go("fb", rs2s.at[part[1]], rel.at[1], y_dn)

    for name in ("x2a", "x2b", "x2c", "x2d"):
        got(name)
    got("fa")
    go("ga", rel.at[0], rs2r.at[part[0]], y_up)
    got("fb")
    go("gb", rel.at[1], rs2r.at[part[1]], y_dn)
    top = pown[0:HALF] + xr2[0].astype(F32) + xr2[2].astype(F32)
    low = pown[HALF:GROUP] + xr2[1].astype(F32) + xr2[3].astype(F32)
    row = lax.broadcasted_iota(jnp.int32, (GROUP, GROUP), 0)
    col = lax.broadcasted_iota(jnp.int32, (GROUP, GROUP), 1)
    twelve = lax.shift_right_logical(row * 5462, 16)
    turn = one_hot((twelve & 3) * 48 + lax.shift_right_logical(twelve, 2) * 12 + row - twelve * 12 == col)
    turned = dot(turn[:, :HALF], top.astype(BF16), 1, 0) + dot(turn[:, HALF:], low.astype(BF16), 1, 0)
    ys[...] = turned.astype(BF16).reshape(4, 48, LANES)
    for d in (2, 1, 3):
        go(f"y{d}", ys.at[lax.rem(yl + d, 4)], yr.at[d - 1], y_of[d])
    total = ys[yl].astype(F32)
    for d in (1, 3, 2):
        got(f"y{d}")
        total += yr[d - 1].astype(F32)

    row = lax.broadcasted_iota(jnp.int32, (64, 48), 0)
    col = lax.broadcasted_iota(jnp.int32, (64, 48), 1)
    inner = row & 7
    spread = one_hot((lax.shift_right_logical(row, 3) * 6 + inner == col) & (inner < 6))
    zs[...] = dot(spread, total.astype(BF16), 1, 0).astype(BF16).reshape(8, 8, LANES)
    for d in (4, 3, 5, 2, 6, 1, 7):
        go(f"z{d}", zs.at[lax.rem(z + d, 8)], zr.at[d - 1], z_of[d])

    got("ga")
    got("gb")
    gin_ref[...] = g_ref[...] + (rf[yh * 2 + c] + rs1r[yh].astype(F32) + rs2r[...].astype(F32))

    total = zs[z].astype(F32)
    for d in (1, 7, 2, 6, 3, 5, 4):
        got(f"z{d}")
        total += zr[d - 1].astype(F32)
    total = total * scale
    for t in range(3):
        gw_ref[t] = total[0:6, GROUP * t : GROUP * (t + 1)]

    for name in NAMES:
        live[name].wait_send()


def shards(inputs, weight, grad_out):
    scale = (inputs.shape[1] * lax.axis_size("seq")) ** (-0.5)
    vmem = pl.BlockSpec(memory_space=pltpu.VMEM)
    count = len(NAMES)

    def body(*refs):
        kernel(scale, *refs)

    return pl.pallas_call(
        body,
        out_shape=(
            jax.ShapeDtypeStruct((GROUP, COLS), F32),
            jax.ShapeDtypeStruct((GROUP, COLS), F32),
            jax.ShapeDtypeStruct((3, 6, GROUP), F32),
        ),
        in_specs=[vmem] * 3,
        out_specs=(vmem,) * 3,
        scratch_shapes=[
            pltpu.VMEM((3, 4, GROUP, COLS), BF16),
            pltpu.VMEM((3, GROUP, 768), BF16),
            pltpu.VMEM((3, GROUP, COLS), BF16),
            pltpu.VMEM((896, COLS), BF16),
            pltpu.VMEM((4, GROUP, LANES), BF16),
            pltpu.VMEM((GROUP, LANES), F32),
            pltpu.VMEM((2, HALF, LANES), BF16),
            pltpu.VMEM((2, HALF, LANES), BF16),
            pltpu.VMEM((4, HALF, LANES), BF16),
            pltpu.VMEM((4, 48, LANES), BF16),
            pltpu.VMEM((3, 48, LANES), BF16),
            pltpu.VMEM((8, 8, LANES), BF16),
            pltpu.VMEM((7, 8, LANES), BF16),
            pltpu.VMEM((4, GROUP, COLS), F32),
            pltpu.VMEM((4, GROUP, COLS), BF16),
            pltpu.VMEM((2, GROUP, COLS), BF16),
            pltpu.VMEM((GROUP, COLS), BF16),
            pltpu.VMEM((2, HALF, COLS), BF16),
            pltpu.VMEM((GROUP, COLS), BF16),
            pltpu.SemaphoreType.DMA((count,)),
            pltpu.SemaphoreType.DMA((count,)),
        ],
        compiler_params=pltpu.CompilerParams(collective_id=0, has_side_effects=True),
    )(inputs, weight, grad_out)


def solution(mesh):
    return jax.shard_map(
        shards,
        mesh=mesh,
        in_specs=(P("ch", "seq"), P(None, "ch", None), P("ch", "seq")),
        out_specs=(P("ch", "seq"), P("ch", "seq"), P(None, "seq", "ch")),
        check_vma=False,
    )
```

```python
import math

import jax
import jax.numpy as jnp
from jax import lax
from jax.experimental import pallas as pl
from jax.experimental.pallas import tpu as pltpu
from jax.sharding import PartitionSpec as P

MESH = pl.DeviceIdType.MESH
F32, BF16 = jnp.float32, jnp.bfloat16
GROUP = 192
HALF = GROUP // 2
COLS = 256
WIDE = 384
LAST = 256

NAMES = []
for k in range(2):
    NAMES += [f"{n}{k}" for n in ("own", "up", "dn", "zu", "zd", "cup", "cdn", "czu", "czd", "cr", "dy", "dz")]
NAMES += ["rup", "rdn", "near", "far", "away", "co", "cf", "ci", "ct"]
for d in range(1, 4):
    NAMES += [f"{n}{d}" for n in ("so", "sf", "si", "st", "dx", "ya", "yb")]
for d in range(1, 8):
    NAMES += [f"za{d}", f"zb{d}"]
SLOT = {name: i for i, name in enumerate(NAMES)}


def dot(a, b, ca, cb):
    return lax.dot_general(a, b, (((ca,), (cb,)), ((), ())), preferred_element_type=F32)


def one_hot(hit):
    return jnp.where(hit, 1.0, 0.0).astype(BF16)


def grid(rows, cols):
    return [lax.broadcasted_iota(jnp.int32, (rows, cols), axis) for axis in range(2)]


def over(value, factor, bits):
    return lax.shift_right_logical(value * factor, bits)


def kernel(
    x_ref, w_ref, g_ref, act_ref, sum_ref, gw_ref,
    xb, xs, wp, wt, db, dx, dlow, ya, yar, za, zar, zb, zbr, yb, ybr, rf, rb, rr, far_s, far_r, send, recv,
):
    s, ch = lax.axis_index("seq"), lax.axis_index("ch")
    z, yl, x = lax.div(s, 16), lax.rem(lax.div(s, 4), 4), lax.rem(s, 4)
    yh, c = lax.div(ch, 2), lax.rem(ch, 2)
    y = yh * 4 + yl
    late = lax.div(yl, 2)

    def at(z, y, x, c):
        z, y, x = lax.rem(z, 8), lax.rem(y, 8), lax.rem(x, 4)
        return (z * 16 + lax.rem(y, 4) * 4 + x, lax.div(y, 4) * 2 + c)

    core = at(z, y, x, 1 - c)
    y_up, y_dn, y_far = at(z, y + 2, x, c), at(z, y + 6, x, c), at(z, y + 4, x, c)
    y_in = at(z, yh * 4 + lax.rem(yl + 2, 4), x, c)
    z_to = at(z + 1 + 6 * late, y, x, c)
    x_of = [None] + [at(z, y, x + d, c) for d in range(1, 4)]
    y_of = [None] + [at(z, yh * 4 + lax.rem(yl + d, 4), x, c) for d in range(1, 4)]
    z_of = [None] + [at(z + d, y, x, c) for d in range(1, 8)]

    barrier = pltpu.get_barrier_semaphore()
    peers = [core, y_up, y_dn, y_far] + x_of[1:] + y_of[1:] + z_of[1:]
    for peer in peers:
        pl.semaphore_signal(barrier, inc=1, device_id=peer, device_id_type=MESH)

    live = {}

    def go(name, src, dst, to):
        i = SLOT[name]
        live[name] = pltpu.make_async_remote_copy(
            src_ref=src, dst_ref=dst, send_sem=send.at[i], recv_sem=recv.at[i], device_id=to, device_id_type=MESH
        )
        live[name].start()

    def got(*names):
        for name in names:
            live[name].wait_recv()

    row, col = grid(WIDE, WIDE)
    upper = jnp.where(row >= GROUP, 1, 0)
    r = row - GROUP * upper
    six = over(r, 10923, 16)
    source = (six & 1) * 96 + (over(six, 1, 1) & 3) * 24 + over(six, 1, 3) * 6 + r - six * 6
    order = one_hot(source + GROUP * upper == col)
    lowered = x_ref[...].astype(BF16)
    xb[1, yh, c] = dot(order[:GROUP, :GROUP], lowered, 1, 0).astype(BF16)

    pl.semaphore_wait(barrier, len(peers))

    t_to = 2 * late
    t_in = 2 - 2 * late
    part = [pl.ds(HALF * k, HALF) for k in range(2)]
    h_dn, h_up, h_far = lax.div(lax.rem(y + 6, 8), 4), lax.div(lax.rem(y + 2, 8), 4), 1 - yh
    for k in range(2):
        mine = xb.at[1, yh, c, part[k]]
        go(f"up{k}", mine, xb.at[t_to, yh, c, part[k]], y_up)
        mine = xb.at[1, yh, c, part[1 - k]]
        go(f"dn{1 - k}", mine, xb.at[t_to, yh, c, part[1 - k]], y_dn)
    for k in range(2):
        mine = xb.at[1, yh, c, part[k]]
        go(f"own{k}", mine, mine, core)

    def slices(d):
        return pl.ds(pl.multiple_of(lax.rem(x + d, 4) * 48, 48), 48)

    for d in (1, 3, 2):
        go(f"so{d}", xb.at[1, yh, c, slices(d)], xs.at[1, d, yh, c], x_of[d])

    for t in range(3):
        for b in range(2):
            cols = slice(WIDE * b, WIDE * (b + 1))
            wp[t, :, cols] = dot(w_ref[t, :, cols], order, 1, 1).astype(BF16)

    for k in range(2):
        got(f"up{k}")
        block = xb.at[t_in, h_dn, c, part[k]]
        go(f"zu{k}", block, xb.at[t_to, h_dn, c, part[k]], z_to)
        if k == 0:
            go("rup", block, xb.at[1, h_dn, c, part[k]], y_up)
        got(f"dn{1 - k}")
        other = xb.at[t_in, h_up, c, part[1 - k]]
        go(f"zd{1 - k}", other, xb.at[t_to, h_up, c, part[1 - k]], z_to)
        if k == 0:
            go("rdn", other, xb.at[1, h_up, c, part[1 - k]], y_dn)
        go(f"cup{k}", block, block, core)
        go(f"cdn{1 - k}", other, other, core)
    for d in (1, 3, 2):
        go(f"si{d}", xb.at[t_in, :, c, slices(d)], xs.at[t_in, d, :, c], x_of[d])
    wide = w_ref[...]
    for t in range(3):
        wt[t] = wide[t].T.reshape(4, GROUP, GROUP)
    got("so1", "so3", "so2")
    go("co", xs.at[1, 1:4, yh, c], xs.at[1, 1:4, yh, c], core)
    for k in range(2):
        got(f"zu{k}")
        block = xb.at[t_to, h_dn, c, part[k]]
        go(f"czu{k}", block, block, core)
        got(f"zd{1 - k}")
        block = xb.at[t_to, h_up, c, part[1 - k]]
        go(f"czd{1 - k}", block, block, core)
        got(("rup", "rdn")[k])
        block = xb.at[1, h_far, c, part[k]]
        go(f"cr{k}", block, block, core)
    for d in (1, 3, 2):
        go(f"st{d}", xb.at[t_to, :, c, slices(d)], xs.at[t_to, d, :, c], x_of[d])
        go(f"sf{d}", xb.at[1, h_far, c, slices(d)], xs.at[1, d, h_far, c], x_of[d])

    def tap(t):
        return dot(wp[t], xb[t].reshape(768, COLS), 1, 0)

    edge = jnp.where((s < 8) | (s >= 120), 0.0, 1.0).astype(F32)
    for k in range(2):
        got(*[f"{name}{k}" for name in ("own", "cup", "cdn", "cr")])
    preact = tap(1) + tap(t_in)
    got("czu0", "czd1", "czu1", "czd0")
    preact += tap(t_to) * edge
    cdf = 0.5 * (1.0 + lax.erf(preact * (1.0 / math.sqrt(2.0))))
    pdf = jnp.exp(-0.5 * preact * preact) * (1.0 / math.sqrt(2.0 * math.pi))
    delta = (g_ref[...] * (cdf + preact * pdf)).astype(BF16)
    db[1] = delta
    dx[0, 0:GROUP] = delta

    for k in range(2):
        go(f"dy{k}", db.at[1, part[k]], db.at[t_to, part[k]], y_in)
    for d in (1, 3, 2):
        go(f"dx{d}", db.at[1], dx.at[d, 0:GROUP], x_of[d])
    act_ref[...] = preact * cdf
    got("si1", "si3", "si2")
    go("ci", xs.at[t_in, 1:4, :, c], xs.at[t_in, 1:4, :, c], core)
    got("sf1", "sf3", "sf2")
    go("cf", xs.at[1, 1:4, h_far, c], xs.at[1, 1:4, h_far, c], core)
    got("st1", "st3", "st2")
    go("ct", xs.at[t_to, 1:4, :, c], xs.at[t_to, 1:4, :, c], core)

    blocks = [(1 - yh) * 2 + 1 - c, (1 - yh) * 2 + c, yh * 2 + 1 - c, yh * 2 + c]
    for i, q in enumerate(blocks):
        rf[i] = dot(wt[1, q], delta, 1, 0)
    for d in range(4):
        dx[d, GROUP:COLS] = jnp.zeros((COLS - GROUP, COLS), BF16)
        dlow[d, 0:GROUP] = jnp.zeros((GROUP, COLS), BF16)
    for k in range(2):
        got(f"dy{k}")
        go(f"dz{k}", db.at[t_in, part[k]], db.at[t_to, part[k]], z_to)
    for i, q in enumerate(blocks):
        rf[i] += dot(wt[2 - t_in, q], db[t_in], 1, 0)

    first = jnp.where(s < 8, 0.0, 1.0).astype(F32)
    last = jnp.where(s >= 120, 0.0, 1.0).astype(F32)
    own_rows = slices(0)
    got("co", "ci", "cf", "ct")
    sums = None
    for d in (0, 1, 3, 2):
        if d:
            got(f"dx{d}")
        dlow[d, GROUP:COLS] = dx[d, 0:64]
        taps = [(xb[t, :, :, own_rows, :] if d == 0 else xs[t, d]).reshape(GROUP, COLS) for t in range(3)]
        new = [dot(taps[0], dx[d], 1, 1), dot(taps[1], dlow[d], 1, 1), dot(taps[1], dx[d, 64:GROUP], 1, 1), dot(taps[2], dx[d], 1, 1)]
        sums = new if sums is None else [a + b for a, b in zip(sums, new)]

    row, col = grid(GROUP, GROUP)
    twelve = over(row, 5462, 16)
    to_y = one_hot((twelve & 3) * 48 + over(twelve, 1, 2) * 12 + row - twelve * 12 == col)
    six = over(row, 10923, 16)
    at_z = over(six, 1, 2)
    to_z = one_hot(over(at_z, 1, 1) * 48 + (six & 3) * 12 + (at_z & 1) * 6 + row - six * 6 == col)

    zb[...] = dot(to_z, (sums[3] * last).astype(BF16), 1, 0).astype(BF16).reshape(8, 24, LAST)
    for d in (4, 3, 5, 2, 6, 1, 7):
        go(f"zb{d}", zb.at[lax.rem(z + d, 8)], zbr.at[d - 1], z_of[d])
    ya[:, :, 0:256] = dot(to_y, (sums[0] * first + sums[1]).astype(BF16), 1, 0).astype(BF16).reshape(4, 48, 256)
    ya[:, :, 256:WIDE] = dot(to_y, sums[2].astype(BF16), 1, 0).astype(BF16).reshape(4, 48, 128)
    for d in (2, 1, 3):
        go(f"ya{d}", ya.at[lax.rem(yl + d, 4)], yar.at[d - 1], y_of[d])

    got("dz0", "dz1")
    for i, q in enumerate(blocks):
        back = rf[i] + dot(wt[2 - t_to, q], db[t_to], 1, 0) * edge
        if i in (0, 2):
            rb[i // 2] = back.astype(BF16)
            go(("far", "near")[i // 2], rb.at[i // 2], rr.at[i // 2], core)
        else:
            rf[i] = back
    got("far")
    far_s[...] = (rf[1] + rr[0].astype(F32)).astype(BF16)
    go("away", far_s, far_r, y_far)

    row, col = grid(64, 48)
    inner = row & 7
    spread = one_hot((over(row, 1, 3) * 6 + inner == col) & (inner < 6))
    total = ya[yl].astype(F32)
    for d in (1, 3, 2):
        got(f"ya{d}")
        total += yar[d - 1].astype(F32)
    za[...] = dot(spread, total.astype(BF16), 1, 0).astype(BF16).reshape(8, 8, WIDE)
    for d in (4, 3, 5, 2, 6, 1, 7):
        go(f"za{d}", za.at[lax.rem(z + d, 8)], zar.at[d - 1], z_of[d])
    total = zb[z].astype(F32)
    for d in (1, 7, 2, 6, 3, 5, 4):
        got(f"zb{d}")
        total += zbr[d - 1].astype(F32)
    yb[...] = dot(spread[0:32, 0:24], total.astype(BF16), 1, 0).astype(BF16).reshape(4, 8, LAST)
    for d in (2, 1, 3):
        go(f"yb{d}", yb.at[lax.rem(yl + d, 4)], ybr.at[d - 1], y_of[d])

    got("near", "away")
    sum_ref[...] = rf[3] + rr[1].astype(F32) + far_r[...].astype(F32)
    total = yb[yl].astype(F32)
    for d in (1, 3, 2):
        got(f"yb{d}")
        total += ybr[d - 1].astype(F32)
    gw_ref[2] = total[0:6, 0:GROUP]
    total = za[z].astype(F32)
    for d in (1, 7, 2, 6, 3, 5, 4):
        got(f"za{d}")
        total += zar[d - 1].astype(F32)
    for t in range(2):
        gw_ref[t] = total[0:6, GROUP * t : GROUP * (t + 1)]

    for name in NAMES:
        live[name].wait_send()


def shards(inputs, weight, grad_out):
    vmem = pl.BlockSpec(memory_space=pltpu.VMEM)
    count = len(NAMES)
    act, total, grad_weight = pl.pallas_call(
        kernel,
        out_shape=(
            jax.ShapeDtypeStruct((GROUP, COLS), F32),
            jax.ShapeDtypeStruct((GROUP, COLS), F32),
            jax.ShapeDtypeStruct((3, 6, GROUP), F32),
        ),
        in_specs=[vmem] * 3,
        out_specs=(vmem,) * 3,
        scratch_shapes=[
            pltpu.VMEM((3, 2, 2, GROUP, COLS), BF16),
            pltpu.VMEM((3, 4, 2, 2, 48, COLS), BF16),
            pltpu.VMEM((3, GROUP, 768), BF16),
            pltpu.VMEM((3, 4, GROUP, GROUP), BF16),
            pltpu.VMEM((3, GROUP, COLS), BF16),
            pltpu.VMEM((4, COLS, COLS), BF16),
            pltpu.VMEM((4, COLS, COLS), BF16),
            pltpu.VMEM((4, 48, WIDE), BF16),
            pltpu.VMEM((3, 48, WIDE), BF16),
            pltpu.VMEM((8, 8, WIDE), BF16),
            pltpu.VMEM((7, 8, WIDE), BF16),
            pltpu.VMEM((8, 24, LAST), BF16),
            pltpu.VMEM((7, 24, LAST), BF16),
            pltpu.VMEM((4, 8, LAST), BF16),
            pltpu.VMEM((3, 8, LAST), BF16),
            pltpu.VMEM((4, GROUP, COLS), F32),
            pltpu.VMEM((2, GROUP, COLS), BF16),
            pltpu.VMEM((2, GROUP, COLS), BF16),
            pltpu.VMEM((GROUP, COLS), BF16),
            pltpu.VMEM((GROUP, COLS), BF16),
            pltpu.SemaphoreType.DMA((count,)),
            pltpu.SemaphoreType.DMA((count,)),
        ],
        compiler_params=pltpu.CompilerParams(collective_id=0, has_side_effects=True),
    )(inputs, weight, grad_out)
    scale = (inputs.shape[1] * lax.axis_size("seq")) ** (-0.5)
    return (inputs + act, grad_out + total, grad_weight * scale)


def solution(mesh):
    return jax.shard_map(
        shards,
        mesh=mesh,
        in_specs=(P("ch", "seq"), P(None, "ch", None), P("ch", "seq")),
        out_specs=(P("ch", "seq"), P("ch", "seq"), P(None, "seq", "ch")),
        check_vma=False,
    )
```

```python
import math

import jax
import jax.numpy as jnp
from jax import lax
from jax.experimental import pallas as pl
from jax.experimental.pallas import tpu as pltpu
from jax.sharding import PartitionSpec as P

MESH = pl.DeviceIdType.MESH
F32, BF16 = jnp.float32, jnp.bfloat16
GROUP = 192
HALF = GROUP // 2
COLS = 256
WIDE = 384
LAST = 256
CHUNKS = 4
CHUNK = GROUP // CHUNKS

NAMES = ["own", "near", "co", "cf", "ci", "ct"]
for k in range(CHUNKS):
    NAMES += [f"{n}{k}" for n in ("up", "dn", "zu", "zd", "cup", "cdn", "czu", "czd", "r", "cr")]
for k in range(2):
    NAMES += [f"{n}{k}" for n in ("dy", "dz", "far", "away")]
for d in range(1, 4):
    NAMES += [f"{n}{d}" for n in ("so", "sf", "si", "st", "dx", "ya", "yb")]
for d in range(1, 8):
    NAMES += [f"za{d}", f"zb{d}"]
SLOT = {name: i for i, name in enumerate(NAMES)}


def dot(a, b, ca, cb):
    return lax.dot_general(a, b, (((ca,), (cb,)), ((), ())), preferred_element_type=F32)


def one_hot(hit):
    return jnp.where(hit, 1.0, 0.0).astype(BF16)


def grid(rows, cols):
    return [lax.broadcasted_iota(jnp.int32, (rows, cols), axis) for axis in range(2)]


def over(value, factor, bits):
    return lax.shift_right_logical(value * factor, bits)


def kernel(
    scale, x_hbm, w_hbm, g_hbm, out_ref, gin_ref, gw_ref,
    x_ref, w_ref, g_ref, xb, xs, wp, wt, db, dx, dlow, ya, yar, za, zar, zb, zbr, yb, ybr, rf, rb, rr, far_s, far_r, load, send, recv,
):
    loads = [pltpu.make_async_copy(a, b, load.at[i]) for i, (a, b) in enumerate(((x_hbm, x_ref), (w_hbm, w_ref), (g_hbm, g_ref)))]
    for one in loads:
        one.start()
    s, ch = lax.axis_index("seq"), lax.axis_index("ch")
    z, yl, x = lax.div(s, 16), lax.rem(lax.div(s, 4), 4), lax.rem(s, 4)
    yh, c = lax.div(ch, 2), lax.rem(ch, 2)
    y = yh * 4 + yl
    late = lax.div(yl, 2)

    def at(z, y, x, c):
        z, y, x = lax.rem(z, 8), lax.rem(y, 8), lax.rem(x, 4)
        return (z * 16 + lax.rem(y, 4) * 4 + x, lax.div(y, 4) * 2 + c)

    core = at(z, y, x, 1 - c)
    y_up, y_dn, y_far = at(z, y + 2, x, c), at(z, y + 6, x, c), at(z, y + 4, x, c)
    y_in = at(z, yh * 4 + lax.rem(yl + 2, 4), x, c)
    z_to = at(z + 1 + 6 * late, y, x, c)
    x_of = [None] + [at(z, y, x + d, c) for d in range(1, 4)]
    y_of = [None] + [at(z, yh * 4 + lax.rem(yl + d, 4), x, c) for d in range(1, 4)]
    z_of = [None] + [at(z + d, y, x, c) for d in range(1, 8)]

    barrier = pltpu.get_barrier_semaphore()
    peers = [core, y_up, y_dn, y_far] + x_of[1:] + y_of[1:] + z_of[1:]
    for peer in peers:
        pl.semaphore_signal(barrier, inc=1, device_id=peer, device_id_type=MESH)

    live = {}

    def go(name, src, dst, to):
        i = SLOT[name]
        live[name] = pltpu.make_async_remote_copy(
            src_ref=src, dst_ref=dst, send_sem=send.at[i], recv_sem=recv.at[i], device_id=to, device_id_type=MESH
        )
        live[name].start()

    def got(*names):
        for name in names:
            live[name].wait_recv()

    def ordering(size):
        row, col = grid(size, size)
        upper = jnp.where(row >= GROUP, 1, 0)
        r = row - GROUP * upper
        six = over(r, 10923, 16)
        source = (six & 1) * 96 + (over(six, 1, 1) & 3) * 24 + over(six, 1, 3) * 6 + r - six * 6
        return one_hot(source + GROUP * upper == col)

    order = ordering(GROUP)
    loads[0].wait()
    xb[1, yh, c] = dot(order, x_ref[...].astype(BF16), 1, 0).astype(BF16)

    pl.semaphore_wait(barrier, len(peers))

    t_to = 2 * late
    t_in = 2 - 2 * late
    piece = [pl.ds(CHUNK * k, CHUNK) for k in range(CHUNKS)]
    part = [pl.ds(HALF * k, HALF) for k in range(2)]
    h_dn, h_up, h_far = lax.div(lax.rem(y + 6, 8), 4), lax.div(lax.rem(y + 2, 8), 4), 1 - yh
    pairs = [(k, CHUNKS - 1 - k) for k in range(CHUNKS)]
    for k, m in pairs:
        go(f"up{k}", xb.at[1, yh, c, piece[k]], xb.at[t_to, yh, c, piece[k]], y_up)
        go(f"dn{m}", xb.at[1, yh, c, piece[m]], xb.at[t_to, yh, c, piece[m]], y_dn)
    go("own", xb.at[1, yh, c], xb.at[1, yh, c], core)

    def slices(d):
        return pl.ds(pl.multiple_of(lax.rem(x + d, 4) * 48, 48), 48)

    for d in (1, 3, 2):
        go(f"so{d}", xb.at[1, yh, c, slices(d)], xs.at[1, d, yh, c], x_of[d])

    order = ordering(WIDE)
    loads[1].wait()
    loads[2].wait()
    for t in range(3):
        for b in range(2):
            cols = slice(WIDE * b, WIDE * (b + 1))
            wp[t, :, cols] = dot(w_ref[t, :, cols], order, 1, 1).astype(BF16)

    for k, m in pairs:
        got(f"up{k}")
        block = xb.at[t_in, h_dn, c, piece[k]]
        go(f"zu{k}", block, xb.at[t_to, h_dn, c, piece[k]], z_to)
        if k < m:
            go(f"r{k}", block, xb.at[1, h_dn, c, piece[k]], y_up)
        got(f"dn{m}")
        other = xb.at[t_in, h_up, c, piece[m]]
        go(f"zd{m}", other, xb.at[t_to, h_up, c, piece[m]], z_to)
        if k < m:
            go(f"r{m}", other, xb.at[1, h_up, c, piece[m]], y_dn)
        go(f"cup{k}", block, block, core)
        go(f"cdn{m}", other, other, core)
    for d in (1, 3, 2):
        go(f"si{d}", xb.at[t_in, :, c, slices(d)], xs.at[t_in, d, :, c], x_of[d])
    wide = w_ref[...]
    for t in range(3):
        wt[t] = wide[t].T.reshape(4, GROUP, GROUP)
    got("so1", "so3", "so2")
    go("co", xs.at[1, 1:4, yh, c], xs.at[1, 1:4, yh, c], core)
    for k, m in pairs:
        got(f"zu{k}")
        block = xb.at[t_to, h_dn, c, piece[k]]
        go(f"czu{k}", block, block, core)
        got(f"zd{m}")
        block = xb.at[t_to, h_up, c, piece[m]]
        go(f"czd{m}", block, block, core)
        if k < m:
            for n in (k, m):
                got(f"r{n}")
                block = xb.at[1, h_far, c, piece[n]]
                go(f"cr{n}", block, block, core)
    for d in (1, 3, 2):
        go(f"st{d}", xb.at[t_to, :, c, slices(d)], xs.at[t_to, d, :, c], x_of[d])
        go(f"sf{d}", xb.at[1, h_far, c, slices(d)], xs.at[1, d, h_far, c], x_of[d])

    def tap(t):
        return dot(wp[t], xb[t].reshape(768, COLS), 1, 0)

    edge = jnp.where((s < 8) | (s >= 120), 0.0, 1.0).astype(F32)
    got("own", *[f"{name}{k}" for k in range(CHUNKS) for name in ("cup", "cdn", "cr")])
    preact = tap(1) + tap(t_in)
    got(*[f"{name}{k}" for k in range(CHUNKS) for name in ("czu", "czd")])
    preact += tap(t_to) * edge
    cdf = 0.5 * (1.0 + lax.erf(preact * (1.0 / math.sqrt(2.0))))
    pdf = jnp.exp(-0.5 * preact * preact) * (1.0 / math.sqrt(2.0 * math.pi))
    delta = (g_ref[...] * (cdf + preact * pdf)).astype(BF16)
    db[1] = delta
    dx[0, 0:GROUP] = delta

    for k in range(2):
        go(f"dy{k}", db.at[1, part[k]], db.at[t_to, part[k]], y_in)
    for d in (1, 3, 2):
        go(f"dx{d}", db.at[1], dx.at[d, 0:GROUP], x_of[d])
    out_ref[...] = x_ref[...] + preact * cdf
    got("si1", "si3", "si2")
    go("ci", xs.at[t_in, 1:4, :, c], xs.at[t_in, 1:4, :, c], core)
    got("sf1", "sf3", "sf2")
    go("cf", xs.at[1, 1:4, h_far, c], xs.at[1, 1:4, h_far, c], core)
    got("st1", "st3", "st2")
    go("ct", xs.at[t_to, 1:4, :, c], xs.at[t_to, 1:4, :, c], core)

    blocks = [(1 - yh) * 2 + 1 - c, (1 - yh) * 2 + c, yh * 2 + 1 - c, yh * 2 + c]
    for i, q in enumerate(blocks):
        rf[i] = dot(wt[1, q], delta, 1, 0)
    for d in range(4):
        dx[d, GROUP:COLS] = jnp.zeros((COLS - GROUP, COLS), BF16)
        dlow[d, 0:GROUP] = jnp.zeros((GROUP, COLS), BF16)
    for k in range(2):
        got(f"dy{k}")
        go(f"dz{k}", db.at[t_in, part[k]], db.at[t_to, part[k]], z_to)
    for i, q in enumerate(blocks):
        rf[i] += dot(wt[2 - t_in, q], db[t_in], 1, 0)

    first = jnp.where(s < 8, 0.0, 1.0).astype(F32)
    last = jnp.where(s >= 120, 0.0, 1.0).astype(F32)
    own_rows = slices(0)
    got("co", "ci", "cf", "ct")
    row, col = grid(GROUP, GROUP)
    twelve = over(row, 5462, 16)
    to_y = one_hot((twelve & 3) * 48 + over(twelve, 1, 2) * 12 + row - twelve * 12 == col)
    six = over(row, 10923, 16)
    at_z = over(six, 1, 2)
    to_z = one_hot(over(at_z, 1, 1) * 48 + (six & 3) * 12 + (at_z & 1) * 6 + row - six * 6 == col)

    def rows_of(t, d):
        return (xb[t, :, :, own_rows, :] if d == 0 else xs[t, d]).reshape(GROUP, COLS)

    sums = None
    for d in (0, 1, 3, 2):
        if d:
            got(f"dx{d}")
        dlow[d, GROUP:COLS] = dx[d, 0:64]
        here = rows_of(1, d)
        new = [dot(rows_of(0, d), dx[d], 1, 1), dot(here, dlow[d], 1, 1), dot(here, dx[d, 64:GROUP], 1, 1)]
        sums = new if sums is None else [a + b for a, b in zip(sums, new)]
    zb[:, :, 0:256] = dot(to_z, (sums[0] * first + sums[1]).astype(BF16), 1, 0).astype(BF16).reshape(8, 24, 256)
    zb[:, :, 256:WIDE] = dot(to_z, sums[2].astype(BF16), 1, 0).astype(BF16).reshape(8, 24, 128)
    for d in (4, 3, 5, 2, 6, 1, 7):
        go(f"zb{d}", zb.at[lax.rem(z + d, 8)], zbr.at[d - 1], z_of[d])
    third = dot(rows_of(2, 0), dx[0], 1, 1)
    for d in range(1, 4):
        third += dot(rows_of(2, d), dx[d], 1, 1)
    ya[...] = dot(to_y, (third * last).astype(BF16), 1, 0).astype(BF16).reshape(4, 48, LAST)
    for d in (2, 1, 3):
        go(f"ya{d}", ya.at[lax.rem(yl + d, 4)], yar.at[d - 1], y_of[d])

    got("dz0", "dz1")
    ends = [dot(wt[2 - t_to, q], db[t_to], 1, 0) * edge for q in blocks[:2]]
    for k in range(2):
        rows = slice(HALF * k, HALF * (k + 1))
        rb[0, rows] = (rf[0, rows] + ends[0][rows]).astype(BF16)
        go(f"far{k}", rb.at[0, part[k]], rr.at[0, part[k]], core)
    for k in range(2):
        rows = slice(HALF * k, HALF * (k + 1))
        mine = rf[1, rows] + ends[1][rows]
        got(f"far{k}")
        far_s[rows] = (mine + rr[0, rows].astype(F32)).astype(BF16)
        go(f"away{k}", far_s.at[part[k]], far_r.at[part[k]], y_far)
    rb[1] = (rf[2] + dot(wt[2 - t_to, blocks[2]], db[t_to], 1, 0) * edge).astype(BF16)
    go("near", rb.at[1], rr.at[1], core)
    rf[3] += dot(wt[2 - t_to, blocks[3]], db[t_to], 1, 0) * edge

    row, col = grid(64, 48)
    inner = row & 7
    spread = one_hot((over(row, 1, 3) * 6 + inner == col) & (inner < 6))
    total = ya[yl].astype(F32)
    for d in (1, 3, 2):
        got(f"ya{d}")
        total += yar[d - 1].astype(F32)
    za[...] = dot(spread, total.astype(BF16), 1, 0).astype(BF16).reshape(8, 8, LAST)
    for d in (4, 3, 5, 2, 6, 1, 7):
        go(f"za{d}", za.at[lax.rem(z + d, 8)], zar.at[d - 1], z_of[d])
    total = zb[z].astype(F32)
    for d in (1, 7, 2, 6, 3, 5, 4):
        got(f"zb{d}")
        total += zbr[d - 1].astype(F32)
    yb[...] = dot(spread[0:32, 0:24], total.astype(BF16), 1, 0).astype(BF16).reshape(4, 8, WIDE)
    for d in (2, 1, 3):
        go(f"yb{d}", yb.at[lax.rem(yl + d, 4)], ybr.at[d - 1], y_of[d])

    got("near", "away0", "away1")
    gin_ref[...] = g_ref[...] + (rf[3] + rr[1].astype(F32) + far_r[...].astype(F32))
    total = yb[yl].astype(F32)
    for d in (1, 3, 2):
        got(f"yb{d}")
        total += ybr[d - 1].astype(F32)
    total = total * scale
    for t in range(2):
        gw_ref[t] = total[0:6, GROUP * t : GROUP * (t + 1)]
    total = za[z].astype(F32)
    for d in (1, 7, 2, 6, 3, 5, 4):
        got(f"za{d}")
        total += zar[d - 1].astype(F32)
    gw_ref[2] = total[0:6, 0:GROUP] * scale

    for name in NAMES:
        live[name].wait_send()


def leave(*refs):
    held, left, done = refs[:3], refs[3:6], refs[6]
    copies = [pltpu.make_async_copy(a, b, done.at[i]) for i, (a, b) in enumerate(zip(held, left))]
    for one in copies:
        one.start()
    for one in copies:
        one.wait()


def shards(inputs, weight, grad_out):
    scale = (inputs.shape[1] * lax.axis_size("seq")) ** (-0.5)
    vmem, hbm = pl.BlockSpec(memory_space=pltpu.VMEM), pl.BlockSpec(memory_space=pltpu.HBM)
    count = len(NAMES)
    shapes = (
        jax.ShapeDtypeStruct((GROUP, COLS), F32),
        jax.ShapeDtypeStruct((GROUP, COLS), F32),
        jax.ShapeDtypeStruct((3, 6, GROUP), F32),
    )

    def body(*refs):
        kernel(scale, *refs)

    held = pl.pallas_call(
        body,
        out_shape=shapes,
        in_specs=[hbm] * 3,
        out_specs=(vmem,) * 3,
        scratch_shapes=[
            pltpu.VMEM((GROUP, COLS), F32),
            pltpu.VMEM((3, GROUP, 768), BF16),
            pltpu.VMEM((GROUP, COLS), F32),
            pltpu.VMEM((3, 2, 2, GROUP, COLS), BF16),
            pltpu.VMEM((3, 4, 2, 2, 48, COLS), BF16),
            pltpu.VMEM((3, GROUP, 768), BF16),
            pltpu.VMEM((3, 4, GROUP, GROUP), BF16),
            pltpu.VMEM((3, GROUP, COLS), BF16),
            pltpu.VMEM((4, COLS, COLS), BF16),
            pltpu.VMEM((4, COLS, COLS), BF16),
            pltpu.VMEM((4, 48, LAST), BF16),
            pltpu.VMEM((3, 48, LAST), BF16),
            pltpu.VMEM((8, 8, LAST), BF16),
            pltpu.VMEM((7, 8, LAST), BF16),
            pltpu.VMEM((8, 24, WIDE), BF16),
            pltpu.VMEM((7, 24, WIDE), BF16),
            pltpu.VMEM((4, 8, WIDE), BF16),
            pltpu.VMEM((3, 8, WIDE), BF16),
            pltpu.VMEM((4, GROUP, COLS), F32),
            pltpu.VMEM((2, GROUP, COLS), BF16),
            pltpu.VMEM((2, GROUP, COLS), BF16),
            pltpu.VMEM((GROUP, COLS), BF16),
            pltpu.VMEM((GROUP, COLS), BF16),
            pltpu.SemaphoreType.DMA((3,)),
            pltpu.SemaphoreType.DMA((count,)),
            pltpu.SemaphoreType.DMA((count,)),
        ],
        compiler_params=pltpu.CompilerParams(collective_id=0, has_side_effects=True, vmem_limit_bytes=20 * 2**20),
    )(*(pltpu.with_memory_space_constraint(a, pltpu.HBM) for a in (inputs, weight, grad_out)))
    return pl.pallas_call(
        leave,
        out_shape=shapes,
        in_specs=[vmem] * 3,
        out_specs=(hbm,) * 3,
        scratch_shapes=[pltpu.SemaphoreType.DMA((3,))],
        compiler_params=pltpu.CompilerParams(vmem_limit_bytes=4 * 2**20),
    )(*held)


def solution(mesh):
    return jax.shard_map(
        shards,
        mesh=mesh,
        in_specs=(P("ch", "seq"), P(None, "ch", None), P("ch", "seq")),
        out_specs=(P("ch", "seq"), P("ch", "seq"), P(None, "seq", "ch")),
        check_vma=False,
    )
```

```python
import math

import jax
import jax.numpy as jnp
from jax import lax
from jax.experimental import pallas as pl
from jax.experimental.pallas import tpu as pltpu
from jax.sharding import PartitionSpec as P

MESH = pl.DeviceIdType.MESH
F32, BF16 = jnp.float32, jnp.bfloat16
GROUP = 192
HALF = GROUP // 2
COLS = 256
TILE = 128
WIDE = 384
LAST = 256
CHUNKS = 4
CHUNK = GROUP // CHUNKS

ARRIVALS = [f"{n}{k}" for n in ("up", "dn", "zu", "zd", "r") for k in range(CHUNKS)]
ARRIVALS += [f"{n}{k}" for n in ("dy0", "dy1", "dz", "far") for k in range(2)]
ARRIVALS += ["near", "away", "here", "next", "so", "si", "sf", "st", "co", "ci", "dx", "ya", "yb", "za", "zb"]
DEPARTURES = ["slabs", "rest", "slices", "grads", "sums", "dx", "ya", "yb", "za", "zb"]
ARRIVE = {name: i for i, name in enumerate(ARRIVALS)}
DEPART = {name: i for i, name in enumerate(DEPARTURES)}


def dot(a, b, ca, cb):
    return lax.dot_general(a, b, (((ca,), (cb,)), ((), ())), preferred_element_type=F32)


def one_hot(hit):
    return jnp.where(hit, 1.0, 0.0).astype(BF16)


def grid(rows, cols):
    return [lax.broadcasted_iota(jnp.int32, (rows, cols), axis) for axis in range(2)]


def over(value, factor, bits):
    return lax.shift_right_logical(value * factor, bits)


def kernel(
    scale, x_hbm, w_hbm, g_hbm, out_ref, gin_ref, gw_ref,
    x_ref, w_ref, g_ref, xb, xs, wp, wt, db, dx, dlow, ya, yar, za, zar, zb, zbr, yb, ybr, rf, rb, rr, far_s, far_r, load, send, recv,
):
    loads = [pltpu.make_async_copy(a, b, load.at[i]) for i, (a, b) in enumerate(((x_hbm, x_ref), (w_hbm, w_ref), (g_hbm, g_ref)))]
    loads[0].start()
    s, ch = lax.axis_index("seq"), lax.axis_index("ch")
    z, yl, x = lax.div(s, 16), lax.rem(lax.div(s, 4), 4), lax.rem(s, 4)
    yh, c = lax.div(ch, 2), lax.rem(ch, 2)
    y = yh * 4 + yl
    late = lax.div(yl, 2)

    def at(z, y, x, c):
        z, y, x = lax.rem(z, 8), lax.rem(y, 8), lax.rem(x, 4)
        return (z * 16 + lax.rem(y, 4) * 4 + x, lax.div(y, 4) * 2 + c)

    core = at(z, y, x, 1 - c)
    y_up, y_dn, y_far = at(z, y + 2, x, c), at(z, y + 6, x, c), at(z, y + 4, x, c)
    y_in = at(z, yh * 4 + lax.rem(yl + 2, 4), x, c)
    z_to = at(z + 1 + 6 * late, y, x, c)
    x_of = [None] + [at(z, y, x + d, c) for d in range(1, 4)]
    y_of = [None] + [at(z, yh * 4 + lax.rem(yl + d, 4), x, c) for d in range(1, 4)]
    z_of = [None] + [at(z + d, y, x, c) for d in range(1, 8)]

    barrier = pltpu.get_barrier_semaphore()
    peers = [core, y_up, y_dn, y_far] + x_of[1:] + y_of[1:] + z_of[1:]
    for peer in peers:
        pl.semaphore_signal(barrier, inc=1, device_id=peer, device_id_type=MESH)

    def copy(arrival, departure, src, dst, to):
        return pltpu.make_async_remote_copy(
            src_ref=src,
            dst_ref=dst,
            send_sem=send.at[DEPART[departure]],
            recv_sem=recv.at[ARRIVE[arrival]],
            device_id=to,
            device_id_type=MESH,
        )

    def go(arrival, departure, src, dst, to):
        copy(arrival, departure, src, dst, to).start()

    def got(arrival, whole):
        copy(arrival, "rest", whole, whole, core).wait_recv()

    def left(departure, whole):
        copy("near", departure, whole, whole, core).wait_send()

    def ordering(size):
        row, col = grid(size, size)
        upper = jnp.where(row >= GROUP, 1, 0)
        r = row - GROUP * upper
        six = over(r, 10923, 16)
        source = (over(six, 1, 2) & 1) * 96 + (six & 3) * 24 + over(six, 1, 3) * 6 + r - six * 6
        return one_hot(source + GROUP * upper == col)

    order = ordering(GROUP)
    loads[0].wait()
    loads[1].start()
    loads[2].start()
    xb[1, yh, c] = dot(order, x_ref[...].astype(BF16), 1, 0).astype(BF16)

    pl.semaphore_wait(barrier, len(peers))

    t_to = 2 * late
    t_in = 2 - 2 * late
    piece = [pl.ds(CHUNK * k, CHUNK) for k in range(CHUNKS)]
    part = [pl.ds(HALF * k, HALF) for k in range(2)]
    h_dn, h_up, h_far = lax.div(lax.rem(y + 6, 8), 4), lax.div(lax.rem(y + 2, 8), 4), 1 - yh
    pairs = [(k, CHUNKS - 1 - k) for k in range(CHUNKS)]
    for k, m in pairs:
        go(f"up{k}", "slabs", xb.at[1, yh, c, piece[k]], xb.at[t_to, yh, c, piece[k]], y_up)
        go(f"dn{m}", "slabs", xb.at[1, yh, c, piece[m]], xb.at[t_to, yh, c, piece[m]], y_dn)
    go("here", "rest", xb.at[1, yh, c], xb.at[1, yh, c], core)

    def slices(d):
        return pl.ds(pl.multiple_of(lax.rem(x + d, 4) * 48, 48), 48)

    for d in (1, 3, 2):
        go("so", "slices", xb.at[1, yh, c, slices(d)], xs.at[1, d, yh, c], x_of[d])

    order = ordering(WIDE)
    loads[1].wait()
    loads[2].wait()
    for t in range(3):
        for b in range(2):
            cols = slice(WIDE * b, WIDE * (b + 1))
            wp[t, :, cols] = dot(w_ref[t, :, cols], order, 1, 1).astype(BF16)

    slab_piece = xb.at[0, 0, 0, piece[0]]
    for k, m in pairs:
        got(f"up{k}", slab_piece)
        block = xb.at[t_in, h_dn, c, piece[k]]
        if k < m:
            go(f"r{k}", "rest", block, xb.at[1, h_dn, c, piece[k]], y_up)
        got(f"dn{m}", slab_piece)
        other = xb.at[t_in, h_up, c, piece[m]]
        if k < m:
            go(f"r{m}", "rest", other, xb.at[1, h_up, c, piece[m]], y_dn)
        go(f"zu{k}", "slabs", block, xb.at[t_to, h_dn, c, piece[k]], z_to)
        go(f"zd{m}", "slabs", other, xb.at[t_to, h_up, c, piece[m]], z_to)
        go("here", "slabs", block, block, core)
        go("here", "slabs", other, other, core)
    for d in (1, 3, 2):
        go("si", "slices", xb.at[t_in, :, c, slices(d)], xs.at[t_in, d, :, c], x_of[d])
    wide = w_ref[...]
    for t in range(3):
        wt[t] = wide[t].T.reshape(4, GROUP, GROUP)
    block = xs.at[1, 1:4, yh, c]
    got("so", block)
    go("co", "slices", block, block, core)
    for k, m in pairs:
        if k < m:
            for n in (k, m):
                got(f"r{n}", slab_piece)
                block = xb.at[1, h_far, c, piece[n]]
                go("here", "rest", block, block, core)
        got(f"zu{k}", slab_piece)
        block = xb.at[t_to, h_dn, c, piece[k]]
        go("next", "slabs", block, block, core)
        got(f"zd{m}", slab_piece)
        block = xb.at[t_to, h_up, c, piece[m]]
        go("next", "slabs", block, block, core)
    for d in (1, 3, 2):
        go("st", "slices", xb.at[t_to, :, c, slices(d)], xs.at[t_to, d, :, c], x_of[d])
        go("sf", "slices", xb.at[1, h_far, c, slices(d)], xs.at[1, d, h_far, c], x_of[d])

    def tap(t):
        return dot(wp[t], xb[t].reshape(768, COLS), 1, 0)

    edge = jnp.where((s < 8) | (s >= 120), 0.0, 1.0).astype(F32)
    got("here", xb.at[0])
    preact = tap(1) + tap(t_in)
    got("next", xb.at[0, 0])
    preact += tap(t_to) * edge
    cdf = 0.5 * (1.0 + lax.erf(preact * (1.0 / math.sqrt(2.0))))
    pdf = jnp.exp(-0.5 * preact * preact) * (1.0 / math.sqrt(2.0 * math.pi))
    delta = (g_ref[...] * (cdf + preact * pdf)).astype(BF16)
    for h in range(2):
        db[1, h] = delta[:, TILE * h : TILE * (h + 1)]
    dx[0, 0:GROUP] = delta

    for h in range(2):
        for k in range(2):
            go(f"dy{h}{k}", "grads", db.at[1, h, part[k]], db.at[t_to, h, part[k]], y_in)
    for d in (1, 3, 2):
        go("dx", "dx", dx.at[0, 0:GROUP], dx.at[d, 0:GROUP], x_of[d])
    out_ref[...] = x_ref[...] + preact * cdf
    for arrival, onward, block in (
        ("si", "ci", xs.at[t_in, 1:4, :, c]),
        ("sf", "co", xs.at[1, 1:4, h_far, c]),
        ("st", "ci", xs.at[t_to, 1:4, :, c]),
    ):
        got(arrival, block)
        go(onward, "slices", block, block, core)

    blocks = [(1 - yh) * 2 + 1 - c, (1 - yh) * 2 + c, yh * 2 + 1 - c, yh * 2 + c]
    for i, q in enumerate(blocks):
        back = dot(wt[1, q], delta, 1, 0)
        for h in range(2):
            rf[i, h] = back[:, TILE * h : TILE * (h + 1)]
    for d in range(4):
        dx[d, GROUP:COLS] = jnp.zeros((COLS - GROUP, COLS), BF16)
        dlow[d, 0:GROUP] = jnp.zeros((GROUP, COLS), BF16)
    for h in range(2):
        for k in range(2):
            got(f"dy{h}{k}", db.at[0, 0, part[0]])
            go(f"dz{h}", "grads", db.at[t_in, h, part[k]], db.at[t_to, h, part[k]], z_to)
        for i, q in enumerate(blocks):
            rf[i, h] += dot(wt[2 - t_in, q], db[t_in, h], 1, 0)

    first = jnp.where(s < 8, 0.0, 1.0).astype(F32)
    last = jnp.where(s >= 120, 0.0, 1.0).astype(F32)
    own_rows = slices(0)
    got("co", xs.at[1, 1:4, :, 0])
    got("ci", xs.at[0, 1:4])
    got("dx", dx.at[1:4, 0:GROUP])
    row, col = grid(GROUP, GROUP)
    six = over(row, 10923, 16)
    to_y = one_hot((six & 7) * 24 + over(six, 1, 3) * 6 + row - six * 6 == col)

    def rows_of(t, d):
        return (xb[t, :, :, own_rows, :] if d == 0 else xs[t, d]).reshape(GROUP, COLS)

    sums = None
    for d in (0, 1, 3, 2):
        dlow[d, GROUP:COLS] = dx[d, 0:64]
        here = rows_of(1, d)
        new = [dot(rows_of(0, d), dx[d], 1, 1), dot(here, dlow[d], 1, 1), dot(here, dx[d, 64:GROUP], 1, 1)]
        sums = new if sums is None else [a + b for a, b in zip(sums, new)]
    zb[:, :, 0:256] = (sums[0] * first + sums[1]).astype(BF16).reshape(8, 24, 256)
    zb[:, :, 256:WIDE] = sums[2].astype(BF16).reshape(8, 24, 128)
    for d in (4, 3, 5, 2, 6, 1, 7):
        go("zb", "zb", zb.at[lax.rem(z + d, 8)], zbr.at[d - 1], z_of[d])
    third = dot(rows_of(2, 0), dx[0], 1, 1)
    for d in range(1, 4):
        third += dot(rows_of(2, d), dx[d], 1, 1)
    ya[...] = dot(to_y, (third * last).astype(BF16), 1, 0).astype(BF16).reshape(4, 48, LAST)
    for d in (2, 1, 3):
        go("ya", "ya", ya.at[lax.rem(yl + d, 4)], yar.at[d - 1], y_of[d])

    for h in range(2):
        got(f"dz{h}", db.at[0, h])

        def whole(i):
            return rf[i, h] + dot(wt[2 - t_to, blocks[i]], db[t_to, h], 1, 0) * edge

        rb[0, h] = whole(0).astype(BF16)
        go(f"far{h}", "grads", rb.at[0, h], rr.at[0, h], core)
        mine = whole(1)
        rb[1, h] = whole(2).astype(BF16)
        go("near", "sums", rb.at[1, h], rr.at[1, h], core)
        rf[3, h] = whole(3)
        got(f"far{h}", rr.at[0, h])
        far_s[h] = (mine + rr[0, h].astype(F32)).astype(BF16)
        go("away", "sums", far_s.at[h], far_r.at[h], y_far)

    row, col = grid(64, 48)
    inner = row & 7
    spread = one_hot((over(row, 1, 3) * 6 + inner == col) & (inner < 6))
    total = ya[yl].astype(F32)
    got("ya", yar)
    for d in (1, 3, 2):
        total += yar[d - 1].astype(F32)
    za[...] = dot(spread, total.astype(BF16), 1, 0).astype(BF16).reshape(8, 8, LAST)
    for d in (4, 3, 5, 2, 6, 1, 7):
        go("za", "za", za.at[lax.rem(z + d, 8)], zar.at[d - 1], z_of[d])
    total = zb[z].astype(F32)
    got("zb", zbr)
    for d in (1, 7, 2, 6, 3, 5, 4):
        total += zbr[d - 1].astype(F32)
    yb[...] = dot(spread[0:32, 0:24], total.astype(BF16), 1, 0).astype(BF16).reshape(4, 8, WIDE)
    for d in (2, 1, 3):
        go("yb", "yb", yb.at[lax.rem(yl + d, 4)], ybr.at[d - 1], y_of[d])

    got("near", rr.at[1])
    left("slabs", xb.at[0:2])
    left("rest", xb.at[:, 0, 0])
    left("slices", xs.at[:, 0:3])
    left("dx", dx.at[1:4, 0:GROUP])
    left("grads", db)
    got("away", far_r)
    for h in range(2):
        cols = slice(TILE * h, TILE * (h + 1))
        gin_ref[:, cols] = g_ref[:, cols] + (rf[3, h] + rr[1, h].astype(F32) + far_r[h].astype(F32))
    total = yb[yl].astype(F32)
    got("yb", ybr)
    for d in (1, 3, 2):
        total += ybr[d - 1].astype(F32)
    total = total * scale
    for t in range(2):
        gw_ref[t] = total[0:6, GROUP * t : GROUP * (t + 1)]
    total = za[z].astype(F32)
    got("za", zar)
    for d in (1, 7, 2, 6, 3, 5, 4):
        total += zar[d - 1].astype(F32)
    gw_ref[2] = total[0:6, 0:GROUP] * scale

    left("sums", rr)
    left("ya", yar)
    left("yb", ybr)
    left("za", zar)
    left("zb", zbr)


def leave(*refs):
    held, left, done = refs[:3], refs[3:6], refs[6]
    copies = [pltpu.make_async_copy(a, b, done.at[i]) for i, (a, b) in enumerate(zip(held, left))]
    for one in copies:
        one.start()
    for one in copies:
        one.wait()


def shards(inputs, weight, grad_out):
    scale = (inputs.shape[1] * lax.axis_size("seq")) ** (-0.5)
    vmem, hbm = pl.BlockSpec(memory_space=pltpu.VMEM), pl.BlockSpec(memory_space=pltpu.HBM)
    shapes = (
        jax.ShapeDtypeStruct((GROUP, COLS), F32),
        jax.ShapeDtypeStruct((GROUP, COLS), F32),
        jax.ShapeDtypeStruct((3, 6, GROUP), F32),
    )

    def body(*refs):
        kernel(scale, *refs)

    held = pl.pallas_call(
        body,
        out_shape=shapes,
        in_specs=[hbm] * 3,
        out_specs=(vmem,) * 3,
        scratch_shapes=[
            pltpu.VMEM((GROUP, COLS), F32),
            pltpu.VMEM((3, GROUP, 768), BF16),
            pltpu.VMEM((GROUP, COLS), F32),
            pltpu.VMEM((3, 2, 2, GROUP, COLS), BF16),
            pltpu.VMEM((3, 4, 2, 2, 48, COLS), BF16),
            pltpu.VMEM((3, GROUP, 768), BF16),
            pltpu.VMEM((3, 4, GROUP, GROUP), BF16),
            pltpu.VMEM((3, 2, GROUP, TILE), BF16),
            pltpu.VMEM((4, COLS, COLS), BF16),
            pltpu.VMEM((4, COLS, COLS), BF16),
            pltpu.VMEM((4, 48, LAST), BF16),
            pltpu.VMEM((3, 48, LAST), BF16),
            pltpu.VMEM((8, 8, LAST), BF16),
            pltpu.VMEM((7, 8, LAST), BF16),
            pltpu.VMEM((8, 24, WIDE), BF16),
            pltpu.VMEM((7, 24, WIDE), BF16),
            pltpu.VMEM((4, 8, WIDE), BF16),
            pltpu.VMEM((3, 8, WIDE), BF16),
            pltpu.VMEM((4, 2, GROUP, TILE), F32),
            pltpu.VMEM((2, 2, GROUP, TILE), BF16),
            pltpu.VMEM((2, 2, GROUP, TILE), BF16),
            pltpu.VMEM((2, GROUP, TILE), BF16),
            pltpu.VMEM((2, GROUP, TILE), BF16),
            pltpu.SemaphoreType.DMA((3,)),
            pltpu.SemaphoreType.DMA((len(DEPARTURES),)),
            pltpu.SemaphoreType.DMA((len(ARRIVALS),)),
        ],
        compiler_params=pltpu.CompilerParams(collective_id=0, has_side_effects=True, vmem_limit_bytes=20 * 2**20),
    )(*(pltpu.with_memory_space_constraint(a, pltpu.HBM) for a in (inputs, weight, grad_out)))
    return pl.pallas_call(
        leave,
        out_shape=shapes,
        in_specs=[vmem] * 3,
        out_specs=(hbm,) * 3,
        scratch_shapes=[pltpu.SemaphoreType.DMA((3,))],
        compiler_params=pltpu.CompilerParams(vmem_limit_bytes=4 * 2**20),
    )(*held)


def solution(mesh):
    return jax.shard_map(
        shards,
        mesh=mesh,
        in_specs=(P("ch", "seq"), P(None, "ch", None), P("ch", "seq")),
        out_specs=(P("ch", "seq"), P("ch", "seq"), P(None, "seq", "ch")),
        check_vma=False,
    )
```

```python
import math

import jax
import jax.numpy as jnp
from jax import lax
from jax.experimental import pallas as pl
from jax.experimental.pallas import tpu as pltpu
from jax.sharding import PartitionSpec as P

MESH = pl.DeviceIdType.MESH
F32, BF16 = jnp.float32, jnp.bfloat16
GROUP = 192
HALF = GROUP // 2
COLS = 256
TILE = 128
WIDE = 384
LAST = 256
CHUNKS = 4
CHUNK = GROUP // CHUNKS

ARRIVALS = [f"{n}{k}" for n in ("up", "dn", "zu", "zd", "r") for k in range(CHUNKS)]
ARRIVALS += [f"{n}{k}" for n in ("dy0", "dy1", "dz", "far") for k in range(2)]
ARRIVALS += ["near", "away", "here", "over", "next", "so", "si", "sf", "st", "co", "ci", "dx1", "dx2", "dx3", "ya", "yb", "za", "zb"]
DEPARTURES = ["slabs", "rest", "slices", "grads", "sums", "dx", "ya", "yb", "za", "zb"]
ARRIVE = {name: i for i, name in enumerate(ARRIVALS)}
DEPART = {name: i for i, name in enumerate(DEPARTURES)}


def dot(a, b, ca, cb):
    return lax.dot_general(a, b, (((ca,), (cb,)), ((), ())), preferred_element_type=F32)


def one_hot(hit):
    return jnp.where(hit, 1.0, 0.0).astype(BF16)


def grid(rows, cols):
    return [lax.broadcasted_iota(jnp.int32, (rows, cols), axis) for axis in range(2)]


def over(value, factor, bits):
    return lax.shift_right_logical(value * factor, bits)


def kernel(
    scale, x_hbm, w_hbm, g_hbm, out_ref, gin_ref, gw_ref,
    x_ref, w_ref, g_ref, xb, xs, wp, wt, db, dx, dlow, ya, yar, za, zar, zb, zbr, yb, ybr, rf, rb, rr, far_s, far_r, load, send, recv,
):
    loads = [pltpu.make_async_copy(a, b, load.at[i]) for i, (a, b) in enumerate(((x_hbm, x_ref), (w_hbm, w_ref), (g_hbm, g_ref)))]
    loads[0].start()
    s, ch = lax.axis_index("seq"), lax.axis_index("ch")
    z, yl, x = lax.div(s, 16), lax.rem(lax.div(s, 4), 4), lax.rem(s, 4)
    yh, c = lax.div(ch, 2), lax.rem(ch, 2)
    y = yh * 4 + yl
    late = lax.div(yl, 2)

    def at(z, y, x, c):
        z, y, x = lax.rem(z, 8), lax.rem(y, 8), lax.rem(x, 4)
        return (z * 16 + lax.rem(y, 4) * 4 + x, lax.div(y, 4) * 2 + c)

    core = at(z, y, x, 1 - c)
    y_up, y_dn, y_far = at(z, y + 2, x, c), at(z, y + 6, x, c), at(z, y + 4, x, c)
    y_in = at(z, yh * 4 + lax.rem(yl + 2, 4), x, c)
    z_to = at(z + 1 + 6 * late, y, x, c)
    x_of = [None] + [at(z, y, x + d, c) for d in range(1, 4)]
    y_of = [None] + [at(z, yh * 4 + lax.rem(yl + d, 4), x, c) for d in range(1, 4)]
    z_of = [None] + [at(z + d, y, x, c) for d in range(1, 8)]

    barrier = pltpu.get_barrier_semaphore()
    peers = [core, y_up, y_dn, y_far] + x_of[1:] + y_of[1:] + z_of[1:]
    for peer in peers:
        pl.semaphore_signal(barrier, inc=1, device_id=peer, device_id_type=MESH)

    def copy(arrival, departure, src, dst, to):
        return pltpu.make_async_remote_copy(
            src_ref=src,
            dst_ref=dst,
            send_sem=send.at[DEPART[departure]],
            recv_sem=recv.at[ARRIVE[arrival]],
            device_id=to,
            device_id_type=MESH,
        )

    def go(arrival, departure, src, dst, to):
        copy(arrival, departure, src, dst, to).start()

    def got(arrival, whole):
        copy(arrival, "rest", whole, whole, core).wait_recv()

    def left(departure, whole):
        copy("near", departure, whole, whole, core).wait_send()

    def ordering(size):
        row, col = grid(size, size)
        upper = jnp.where(row >= GROUP, 1, 0)
        r = row - GROUP * upper
        six = over(r, 10923, 16)
        source = (over(six, 1, 2) & 1) * 96 + (six & 3) * 24 + over(six, 1, 3) * 6 + r - six * 6
        return one_hot(source + GROUP * upper == col)

    order = ordering(GROUP)
    loads[0].wait()
    loads[1].start()
    loads[2].start()
    xb[1, yh, c] = dot(order, x_ref[...].astype(BF16), 1, 0).astype(BF16)

    pl.semaphore_wait(barrier, len(peers))

    t_to = 2 * late
    t_in = 2 - 2 * late
    piece = [pl.ds(CHUNK * k, CHUNK) for k in range(CHUNKS)]
    part = [pl.ds(HALF * k, HALF) for k in range(2)]
    h_dn, h_up, h_far = lax.div(lax.rem(y + 6, 8), 4), lax.div(lax.rem(y + 2, 8), 4), 1 - yh
    pairs = [(k, CHUNKS - 1 - k) for k in range(CHUNKS)]
    for k, m in pairs:
        go(f"up{k}", "slabs", xb.at[1, yh, c, piece[k]], xb.at[t_to, yh, c, piece[k]], y_up)
        go(f"dn{m}", "slabs", xb.at[1, yh, c, piece[m]], xb.at[t_to, yh, c, piece[m]], y_dn)
    go("here", "rest", xb.at[1, yh, c], xb.at[1, yh, c], core)

    def slices(d):
        return pl.ds(pl.multiple_of(lax.rem(x + d, 4) * 48, 48), 48)

    for d in (1, 3, 2):
        go("so", "slices", xb.at[1, yh, c, slices(d)], xs.at[1, d, yh, c], x_of[d])

    order = ordering(WIDE)
    loads[1].wait()
    loads[2].wait()
    for t in range(3):
        for b in range(2):
            cols = slice(WIDE * b, WIDE * (b + 1))
            wp[t, :, cols] = dot(w_ref[t, :, cols], order, 1, 1).astype(BF16)

    slab_piece = xb.at[0, 0, 0, piece[0]]
    for k, m in pairs:
        got(f"up{k}", slab_piece)
        block = xb.at[t_in, h_dn, c, piece[k]]
        if k < m:
            go(f"r{k}", "rest", block, xb.at[1, h_dn, c, piece[k]], y_up)
        got(f"dn{m}", slab_piece)
        other = xb.at[t_in, h_up, c, piece[m]]
        if k < m:
            go(f"r{m}", "rest", other, xb.at[1, h_up, c, piece[m]], y_dn)
        go(f"zu{k}", "slabs", block, xb.at[t_to, h_dn, c, piece[k]], z_to)
        go(f"zd{m}", "slabs", other, xb.at[t_to, h_up, c, piece[m]], z_to)
        go("here", "slabs", block, block, core)
        go("here", "slabs", other, other, core)
    for d in (1, 3, 2):
        go("si", "slices", xb.at[t_in, :, c, slices(d)], xs.at[t_in, d, :, c], x_of[d])
    wide = w_ref[...]
    for t in range(3):
        wt[t] = wide[t].T.reshape(4, GROUP, GROUP)
    block = xs.at[1, 1:4, yh, c]
    got("so", block)
    go("co", "slices", block, block, core)
    for k, m in pairs:
        if k < m:
            for n in (k, m):
                got(f"r{n}", slab_piece)
                block = xb.at[1, h_far, c, piece[n]]
                go("over", "rest", block, block, core)
            if k + 1 == m:
                for d in (1, 3, 2):
                    go("sf", "slices", xb.at[1, h_far, c, slices(d)], xs.at[1, d, h_far, c], x_of[d])
        got(f"zu{k}", slab_piece)
        block = xb.at[t_to, h_dn, c, piece[k]]
        go("next", "slabs", block, block, core)
        got(f"zd{m}", slab_piece)
        block = xb.at[t_to, h_up, c, piece[m]]
        go("next", "slabs", block, block, core)
    def tap(t):
        return dot(wp[t], xb[t].reshape(768, COLS), 1, 0)

    edge = jnp.where((s < 8) | (s >= 120), 0.0, 1.0).astype(F32)
    def half(h):
        cols = pl.ds(pl.multiple_of(h * WIDE, TILE), WIDE)
        return dot(wp[1, :, cols], xb[1, h].reshape(WIDE, COLS), 1, 0)

    got("here", xb.at[:, 0, 0])
    preact = half(yh) + tap(t_in)
    got("next", xb.at[0, 0])
    preact += tap(t_to) * edge
    block = xs.at[t_in, 1:4, :, c]
    got("si", block)
    go("st", "slices", block, xs.at[t_to, 1:4, :, c], z_to)
    go("ci", "slices", block, block, core)
    got("over", xb.at[0, 0, 0])
    preact += half(h_far)
    cdf = 0.5 * (1.0 + lax.erf(preact * (1.0 / math.sqrt(2.0))))
    pdf = jnp.exp(-0.5 * preact * preact) * (1.0 / math.sqrt(2.0 * math.pi))
    delta = (g_ref[...] * (cdf + preact * pdf)).astype(BF16)
    for h in range(2):
        db[1, h] = delta[:, TILE * h : TILE * (h + 1)]
    dx[0, 0:GROUP] = delta

    for h in range(2):
        for k in range(2):
            go(f"dy{h}{k}", "grads", db.at[1, h, part[k]], db.at[t_to, h, part[k]], y_in)
    for d in (1, 3, 2):
        go(f"dx{d}", "dx", dx.at[0, 0:GROUP], dx.at[d, 0:GROUP], x_of[d])
    out_ref[...] = x_ref[...] + preact * cdf
    blocks = [(1 - yh) * 2 + 1 - c, (1 - yh) * 2 + c, yh * 2 + 1 - c, yh * 2 + c]
    for i, q in enumerate(blocks):
        back = dot(wt[1, q], delta, 1, 0)
        for h in range(2):
            rf[i, h] = back[:, TILE * h : TILE * (h + 1)]
    for d in range(4):
        dx[d, GROUP:COLS] = jnp.zeros((COLS - GROUP, COLS), BF16)
        dlow[d, 0:GROUP] = jnp.zeros((GROUP, COLS), BF16)
    own_rows = slices(0)

    def rows_of(t, d):
        return (xb[t, :, :, own_rows, :] if d == 0 else xs[t, d]).reshape(GROUP, COLS)

    def products(d):
        dlow[d, GROUP:COLS] = dx[d, 0:64]
        here = rows_of(1, d)
        wide, low, high = dx[d], dlow[d], dx[d, 64:GROUP]
        return [dot(rows_of(0, d), wide, 1, 1), dot(here, low, 1, 1), dot(here, high, 1, 1), dot(rows_of(2, d), wide, 1, 1)]

    sums = products(0)
    for arrival, onward, block in (
        ("sf", "co", xs.at[1, 1:4, h_far, c]),
        ("st", "ci", xs.at[t_to, 1:4, :, c]),
    ):
        got(arrival, block)
        go(onward, "slices", block, block, core)
    for h in range(2):
        for k in range(2):
            got(f"dy{h}{k}", db.at[0, 0, part[0]])
            go(f"dz{h}", "grads", db.at[t_in, h, part[k]], db.at[t_to, h, part[k]], z_to)
        for i, q in enumerate(blocks):
            rf[i, h] += dot(wt[2 - t_in, q], db[t_in, h], 1, 0)

    first = jnp.where(s < 8, 0.0, 1.0).astype(F32)
    last = jnp.where(s >= 120, 0.0, 1.0).astype(F32)
    got("co", xs.at[1, 1:4, :, 0])
    got("ci", xs.at[0, 1:4])
    row, col = grid(GROUP, GROUP)
    six = over(row, 10923, 16)
    to_y = one_hot((six & 7) * 24 + over(six, 1, 3) * 6 + row - six * 6 == col)

    for d in (1, 3, 2):
        got(f"dx{d}", dx.at[1, 0:GROUP])
        sums = [a + b for a, b in zip(sums, products(d))]
    zb[:, :, 0:256] = (sums[0] * first + sums[1]).astype(BF16).reshape(8, 24, 256)
    zb[:, :, 256:WIDE] = sums[2].astype(BF16).reshape(8, 24, 128)
    for d in (4, 3, 5, 2, 6, 1, 7):
        go("zb", "zb", zb.at[lax.rem(z + d, 8)], zbr.at[d - 1], z_of[d])
    ya[...] = dot(to_y, (sums[3] * last).astype(BF16), 1, 0).astype(BF16).reshape(4, 48, LAST)
    for d in (2, 1, 3):
        go("ya", "ya", ya.at[lax.rem(yl + d, 4)], yar.at[d - 1], y_of[d])

    for h in range(2):
        got(f"dz{h}", db.at[0, h])

        def whole(i):
            return rf[i, h] + dot(wt[2 - t_to, blocks[i]], db[t_to, h], 1, 0) * edge

        rb[0, h] = whole(0).astype(BF16)
        go(f"far{h}", "grads", rb.at[0, h], rr.at[0, h], core)
        mine = whole(1)
        rb[1, h] = whole(2).astype(BF16)
        go("near", "sums", rb.at[1, h], rr.at[1, h], core)
        rf[3, h] = whole(3)
        got(f"far{h}", rr.at[0, h])
        far_s[h] = (mine + rr[0, h].astype(F32)).astype(BF16)
        go("away", "sums", far_s.at[h], far_r.at[h], y_far)

    row, col = grid(64, 48)
    inner = row & 7
    spread = one_hot((over(row, 1, 3) * 6 + inner == col) & (inner < 6))
    total = ya[yl].astype(F32)
    got("ya", yar)
    for d in (1, 3, 2):
        total += yar[d - 1].astype(F32)
    za[...] = dot(spread, total.astype(BF16), 1, 0).astype(BF16).reshape(8, 8, LAST)
    for d in (4, 3, 5, 2, 6, 1, 7):
        go("za", "za", za.at[lax.rem(z + d, 8)], zar.at[d - 1], z_of[d])
    total = zb[z].astype(F32)
    got("zb", zbr)
    for d in (1, 7, 2, 6, 3, 5, 4):
        total += zbr[d - 1].astype(F32)
    yb[...] = dot(spread[0:32, 0:24], total.astype(BF16), 1, 0).astype(BF16).reshape(4, 8, WIDE)
    for d in (2, 1, 3):
        go("yb", "yb", yb.at[lax.rem(yl + d, 4)], ybr.at[d - 1], y_of[d])

    got("near", rr.at[1])
    left("slabs", xb.at[0:2])
    left("rest", xb.at[:, 0, 0])
    left("slices", xs.at[:, 0:3])
    left("dx", dx.at[1:4, 0:GROUP])
    left("grads", db)
    got("away", far_r)
    for h in range(2):
        cols = slice(TILE * h, TILE * (h + 1))
        gin_ref[:, cols] = g_ref[:, cols] + (rf[3, h] + rr[1, h].astype(F32) + far_r[h].astype(F32))
    total = yb[yl].astype(F32)
    got("yb", ybr)
    for d in (1, 3, 2):
        total += ybr[d - 1].astype(F32)
    total = total * scale
    for t in range(2):
        gw_ref[t] = total[0:6, GROUP * t : GROUP * (t + 1)]
    total = za[z].astype(F32)
    got("za", zar)
    for d in (1, 7, 2, 6, 3, 5, 4):
        total += zar[d - 1].astype(F32)
    gw_ref[2] = total[0:6, 0:GROUP] * scale

    left("sums", rr)
    left("ya", yar)
    left("yb", ybr)
    left("za", zar)
    left("zb", zbr)


def leave(*refs):
    held, left, done = refs[:3], refs[3:6], refs[6]
    copies = [pltpu.make_async_copy(a, b, done.at[i]) for i, (a, b) in enumerate(zip(held, left))]
    for one in copies:
        one.start()
    for one in copies:
        one.wait()


def shards(inputs, weight, grad_out):
    scale = (inputs.shape[1] * lax.axis_size("seq")) ** (-0.5)
    vmem, hbm = pl.BlockSpec(memory_space=pltpu.VMEM), pl.BlockSpec(memory_space=pltpu.HBM)
    shapes = (
        jax.ShapeDtypeStruct((GROUP, COLS), F32),
        jax.ShapeDtypeStruct((GROUP, COLS), F32),
        jax.ShapeDtypeStruct((3, 6, GROUP), F32),
    )

    def body(*refs):
        kernel(scale, *refs)

    held = pl.pallas_call(
        body,
        out_shape=shapes,
        in_specs=[hbm] * 3,
        out_specs=(vmem,) * 3,
        scratch_shapes=[
            pltpu.VMEM((GROUP, COLS), F32),
            pltpu.VMEM((3, GROUP, 768), BF16),
            pltpu.VMEM((GROUP, COLS), F32),
            pltpu.VMEM((3, 2, 2, GROUP, COLS), BF16),
            pltpu.VMEM((3, 4, 2, 2, 48, COLS), BF16),
            pltpu.VMEM((3, GROUP, 768), BF16),
            pltpu.VMEM((3, 4, GROUP, GROUP), BF16),
            pltpu.VMEM((3, 2, GROUP, TILE), BF16),
            pltpu.VMEM((4, COLS, COLS), BF16),
            pltpu.VMEM((4, COLS, COLS), BF16),
            pltpu.VMEM((4, 48, LAST), BF16),
            pltpu.VMEM((3, 48, LAST), BF16),
            pltpu.VMEM((8, 8, LAST), BF16),
            pltpu.VMEM((7, 8, LAST), BF16),
            pltpu.VMEM((8, 24, WIDE), BF16),
            pltpu.VMEM((7, 24, WIDE), BF16),
            pltpu.VMEM((4, 8, WIDE), BF16),
            pltpu.VMEM((3, 8, WIDE), BF16),
            pltpu.VMEM((4, 2, GROUP, TILE), F32),
            pltpu.VMEM((2, 2, GROUP, TILE), BF16),
            pltpu.VMEM((2, 2, GROUP, TILE), BF16),
            pltpu.VMEM((2, GROUP, TILE), BF16),
            pltpu.VMEM((2, GROUP, TILE), BF16),
            pltpu.SemaphoreType.DMA((3,)),
            pltpu.SemaphoreType.DMA((len(DEPARTURES),)),
            pltpu.SemaphoreType.DMA((len(ARRIVALS),)),
        ],
        compiler_params=pltpu.CompilerParams(collective_id=0, has_side_effects=True, vmem_limit_bytes=20 * 2**20),
    )(*(pltpu.with_memory_space_constraint(a, pltpu.HBM) for a in (inputs, weight, grad_out)))
    return pl.pallas_call(
        leave,
        out_shape=shapes,
        in_specs=[vmem] * 3,
        out_specs=(hbm,) * 3,
        scratch_shapes=[pltpu.SemaphoreType.DMA((3,))],
        compiler_params=pltpu.CompilerParams(vmem_limit_bytes=4 * 2**20),
    )(*held)


def solution(mesh):
    return jax.shard_map(
        shards,
        mesh=mesh,
        in_specs=(P("ch", "seq"), P(None, "ch", None), P("ch", "seq")),
        out_specs=(P("ch", "seq"), P("ch", "seq"), P(None, "seq", "ch")),
        check_vma=False,
    )
```

```python
import math

import jax
import jax.numpy as jnp
from jax import lax
from jax.experimental import pallas as pl
from jax.experimental.pallas import tpu as pltpu
from jax.sharding import PartitionSpec as P

MESH = pl.DeviceIdType.MESH
F32, BF16 = jnp.float32, jnp.bfloat16
GROUP = 192
HALF = GROUP // 2
COLS = 256
TILE = 128
WIDE = 384
LAST = 256
CHUNKS = 4
CHUNK = GROUP // CHUNKS

ARRIVALS = [f"{n}{k}" for n in ("up", "dn", "zu", "zd", "r") for k in range(CHUNKS)]
ARRIVALS += [f"{n}{k}" for n in ("dy0", "dy1", "dz", "far") for k in range(2)]
ARRIVALS += ["near", "away", "here", "over", "next", "so", "si", "sf", "st", "co", "ci", "dx1", "dx2", "dx3", "ya", "yb", "za", "zb"]
DEPARTURES = ["slabs", "rest", "slices", "grads", "sums", "dx", "ya", "yb", "za", "zb"]
ARRIVE = {name: i for i, name in enumerate(ARRIVALS)}
DEPART = {name: i for i, name in enumerate(DEPARTURES)}


def dot(a, b, ca, cb):
    return lax.dot_general(a, b, (((ca,), (cb,)), ((), ())), preferred_element_type=F32)


def one_hot(hit):
    return jnp.where(hit, 1.0, 0.0).astype(BF16)


def grid(rows, cols):
    return [lax.broadcasted_iota(jnp.int32, (rows, cols), axis) for axis in range(2)]


def over(value, factor, bits):
    return lax.shift_right_logical(value * factor, bits)


def kernel(
    scale, x_hbm, w_hbm, g_hbm, out_ref, gin_ref, gw_ref,
    x_ref, w_ref, g_ref, xb, xs, wp, wt, db, dx, dlow, ya, yar, za, zar, zb, zbr, yb, ybr, rf, rb, rr, far_s, far_r, load, send, recv,
):
    loads = [pltpu.make_async_copy(a, b, load.at[i]) for i, (a, b) in enumerate(((x_hbm, x_ref), (w_hbm, w_ref), (g_hbm, g_ref)))]
    loads[0].start()
    s, ch = lax.axis_index("seq"), lax.axis_index("ch")
    z, yl, x = lax.div(s, 16), lax.rem(lax.div(s, 4), 4), lax.rem(s, 4)
    yh, c = lax.div(ch, 2), lax.rem(ch, 2)
    y = yh * 4 + yl
    late = lax.div(yl, 2)

    def at(z, y, x, c):
        z, y, x = lax.rem(z, 8), lax.rem(y, 8), lax.rem(x, 4)
        return (z * 16 + lax.rem(y, 4) * 4 + x, lax.div(y, 4) * 2 + c)

    core = at(z, y, x, 1 - c)
    y_up, y_dn, y_far = at(z, y + 2, x, c), at(z, y + 6, x, c), at(z, y + 4, x, c)
    y_in = at(z, yh * 4 + lax.rem(yl + 2, 4), x, c)
    z_to = at(z + 1 + 6 * late, y, x, c)
    x_of = [None] + [at(z, y, x + d, c) for d in range(1, 4)]
    y_of = [None] + [at(z, yh * 4 + lax.rem(yl + d, 4), x, c) for d in range(1, 4)]
    z_of = [None] + [at(z + d, y, x, c) for d in range(1, 8)]

    barrier = pltpu.get_barrier_semaphore()
    peers = [core, y_up, y_dn, y_far] + x_of[1:] + y_of[1:] + z_of[1:]
    for peer in peers:
        pl.semaphore_signal(barrier, inc=1, device_id=peer, device_id_type=MESH)

    def copy(arrival, departure, src, dst, to):
        return pltpu.make_async_remote_copy(
            src_ref=src,
            dst_ref=dst,
            send_sem=send.at[DEPART[departure]],
            recv_sem=recv.at[ARRIVE[arrival]],
            device_id=to,
            device_id_type=MESH,
        )

    def go(arrival, departure, src, dst, to):
        copy(arrival, departure, src, dst, to).start()

    def got(arrival, whole):
        copy(arrival, "rest", whole, whole, core).wait_recv()

    def left(departure, whole):
        copy("near", departure, whole, whole, core).wait_send()

    def ordering(size):
        row, col = grid(size, size)
        upper = jnp.where(row >= GROUP, 1, 0)
        r = row - GROUP * upper
        six = over(r, 10923, 16)
        source = (over(six, 1, 2) & 1) * 96 + (six & 3) * 24 + over(six, 1, 3) * 6 + r - six * 6
        return one_hot(source + GROUP * upper == col)

    order = ordering(GROUP)
    loads[0].wait()
    loads[1].start()
    loads[2].start()
    xb[1, yh, c] = dot(order, x_ref[...].astype(BF16), 1, 0).astype(BF16)

    pl.semaphore_wait(barrier, len(peers))

    t_to = 2 * late
    t_in = 2 - 2 * late
    piece = [pl.ds(CHUNK * k, CHUNK) for k in range(CHUNKS)]
    part = [pl.ds(HALF * k, HALF) for k in range(2)]
    h_dn, h_up, h_far = lax.div(lax.rem(y + 6, 8), 4), lax.div(lax.rem(y + 2, 8), 4), 1 - yh
    pairs = [(k, CHUNKS - 1 - k) for k in range(CHUNKS)]
    for k, m in pairs:
        go(f"up{k}", "slabs", xb.at[1, yh, c, piece[k]], xb.at[t_to, yh, c, piece[k]], y_up)
        go(f"dn{m}", "slabs", xb.at[1, yh, c, piece[m]], xb.at[t_to, yh, c, piece[m]], y_dn)
    go("here", "rest", xb.at[1, yh, c], xb.at[1, yh, c], core)

    def slices(d):
        return pl.ds(pl.multiple_of(lax.rem(x + d, 4) * 48, 48), 48)

    for d in (1, 3, 2):
        go("so", "slices", xb.at[1, yh, c, slices(d)], xs.at[1, d, yh, c], x_of[d])

    order = ordering(WIDE)
    loads[1].wait()
    loads[2].wait()
    for t in range(3):
        for b in range(2):
            cols = slice(WIDE * b, WIDE * (b + 1))
            wp[t, :, cols] = dot(w_ref[t, :, cols], order, 1, 1).astype(BF16)

    slab_piece = xb.at[0, 0, 0, piece[0]]
    for k, m in pairs:
        got(f"up{k}", slab_piece)
        block = xb.at[t_in, h_dn, c, piece[k]]
        if k < m:
            go(f"r{k}", "rest", block, xb.at[1, h_dn, c, piece[k]], y_up)
        got(f"dn{m}", slab_piece)
        other = xb.at[t_in, h_up, c, piece[m]]
        if k < m:
            go(f"r{m}", "rest", other, xb.at[1, h_up, c, piece[m]], y_dn)
        go(f"zu{k}", "slabs", block, xb.at[t_to, h_dn, c, piece[k]], z_to)
        go(f"zd{m}", "slabs", other, xb.at[t_to, h_up, c, piece[m]], z_to)
        go("here", "slabs", block, block, core)
        go("here", "slabs", other, other, core)
    for d in (1, 3, 2):
        go("si", "slices", xb.at[t_in, :, c, slices(d)], xs.at[t_in, d, :, c], x_of[d])
    wide = w_ref[...]
    for t in range(3):
        wt[t] = wide[t].T.reshape(4, GROUP, GROUP)
    block = xs.at[1, 1:4, yh, c]
    got("so", block)
    go("co", "slices", block, block, core)
    for k, m in pairs:
        if k < m:
            for n in (k, m):
                got(f"r{n}", slab_piece)
                block = xb.at[1, h_far, c, piece[n]]
                go("over", "rest", block, block, core)
            if k + 1 == m:
                for d in (1, 3, 2):
                    go("sf", "slices", xb.at[1, h_far, c, slices(d)], xs.at[1, d, h_far, c], x_of[d])
        got(f"zu{k}", slab_piece)
        block = xb.at[t_to, h_dn, c, piece[k]]
        go("next", "slabs", block, block, core)
        got(f"zd{m}", slab_piece)
        block = xb.at[t_to, h_up, c, piece[m]]
        go("next", "slabs", block, block, core)
    def tap(t):
        return dot(wp[t], xb[t].reshape(768, COLS), 1, 0)

    edge = jnp.where((s < 8) | (s >= 120), 0.0, 1.0).astype(F32)
    def half(h):
        cols = pl.ds(pl.multiple_of(h * WIDE, TILE), WIDE)
        return dot(wp[1, :, cols], xb[1, h].reshape(WIDE, COLS), 1, 0)

    got("here", xb.at[:, 0, 0])
    preact = half(yh) + tap(t_in)
    got("next", xb.at[0, 0])
    preact += tap(t_to) * edge
    block = xs.at[t_in, 1:4, :, c]
    got("si", block)
    go("st", "slices", block, xs.at[t_to, 1:4, :, c], z_to)
    go("ci", "slices", block, block, core)
    got("over", xb.at[0, 0, 0])
    preact += half(h_far)
    cdf = 0.5 * (1.0 + lax.erf(preact * (1.0 / math.sqrt(2.0))))
    pdf = jnp.exp(-0.5 * preact * preact) * (1.0 / math.sqrt(2.0 * math.pi))
    delta = (g_ref[...] * (cdf + preact * pdf)).astype(BF16)
    for h in range(2):
        db[1, h] = delta[:, TILE * h : TILE * (h + 1)]
    dx[0, 0:GROUP] = delta

    for h in range(2):
        for k in range(2):
            go(f"dy{h}{k}", "grads", db.at[1, h, part[k]], db.at[t_to, h, part[k]], y_in)
    for d in (2, 1, 3):
        go(f"dx{d}", "dx", dx.at[0, 0:GROUP], dx.at[d, 0:GROUP], x_of[d])
    out_ref[...] = x_ref[...] + preact * cdf
    blocks = [(1 - yh) * 2 + 1 - c, (1 - yh) * 2 + c, yh * 2 + 1 - c, yh * 2 + c]
    for i, q in enumerate(blocks):
        back = dot(wt[1, q], delta, 1, 0)
        for h in range(2):
            rf[i, h] = back[:, TILE * h : TILE * (h + 1)]
    for d in range(4):
        dx[d, GROUP:COLS] = jnp.zeros((COLS - GROUP, COLS), BF16)
        dlow[d, 0:GROUP] = jnp.zeros((GROUP, COLS), BF16)
    own_rows = slices(0)

    def rows_of(t, d):
        return (xb[t, :, :, own_rows, :] if d == 0 else xs[t, d]).reshape(GROUP, COLS)

    def products(d):
        dlow[d, GROUP:COLS] = dx[d, 0:64]
        here = rows_of(1, d)
        wide, low, high = dx[d], dlow[d], dx[d, 64:GROUP]
        return [dot(rows_of(0, d), wide, 1, 1), dot(here, low, 1, 1), dot(here, high, 1, 1), dot(rows_of(2, d), wide, 1, 1)]

    sums = products(0)
    for arrival, onward, block in (
        ("sf", "co", xs.at[1, 1:4, h_far, c]),
        ("st", "ci", xs.at[t_to, 1:4, :, c]),
    ):
        got(arrival, block)
        go(onward, "slices", block, block, core)
    for h in range(2):
        for k in range(2):
            got(f"dy{h}{k}", db.at[0, 0, part[0]])
            go(f"dz{h}", "grads", db.at[t_in, h, part[k]], db.at[t_to, h, part[k]], z_to)
        for i, q in enumerate(blocks):
            rf[i, h] += dot(wt[2 - t_in, q], db[t_in, h], 1, 0)

    first = jnp.where(s < 8, 0.0, 1.0).astype(F32)
    last = jnp.where(s >= 120, 0.0, 1.0).astype(F32)
    got("co", xs.at[1, 1:4, :, 0])
    got("ci", xs.at[0, 1:4])
    row, col = grid(GROUP, GROUP)
    six = over(row, 10923, 16)
    to_y = one_hot((six & 7) * 24 + over(six, 1, 3) * 6 + row - six * 6 == col)

    for d in (1, 3, 2):
        got(f"dx{d}", dx.at[1, 0:GROUP])
        sums = [a + b for a, b in zip(sums, products(d))]
    zb[:, :, 0:256] = (sums[0] * first + sums[1]).astype(BF16).reshape(8, 24, 256)
    zb[:, :, 256:WIDE] = sums[2].astype(BF16).reshape(8, 24, 128)
    for d in (4, 3, 5, 2, 6, 1, 7):
        go("zb", "zb", zb.at[lax.rem(z + d, 8)], zbr.at[d - 1], z_of[d])
    ya[...] = dot(to_y, (sums[3] * last).astype(BF16), 1, 0).astype(BF16).reshape(4, 48, LAST)
    for d in (2, 1, 3):
        go("ya", "ya", ya.at[lax.rem(yl + d, 4)], yar.at[d - 1], y_of[d])

    for h in range(2):
        got(f"dz{h}", db.at[0, h])

        def whole(i):
            return rf[i, h] + dot(wt[2 - t_to, blocks[i]], db[t_to, h], 1, 0) * edge

        rb[0, h] = whole(0).astype(BF16)
        go(f"far{h}", "grads", rb.at[0, h], rr.at[0, h], core)
        mine = whole(1)
        rb[1, h] = whole(2).astype(BF16)
        go("near", "sums", rb.at[1, h], rr.at[1, h], core)
        rf[3, h] = whole(3)
        got(f"far{h}", rr.at[0, h])
        far_s[h] = (mine + rr[0, h].astype(F32)).astype(BF16)
        go("away", "sums", far_s.at[h], far_r.at[h], y_far)

    row, col = grid(64, 48)
    inner = row & 7
    spread = one_hot((over(row, 1, 3) * 6 + inner == col) & (inner < 6))
    total = ya[yl].astype(F32)
    got("ya", yar)
    for d in (1, 3, 2):
        total += yar[d - 1].astype(F32)
    za[...] = dot(spread, total.astype(BF16), 1, 0).astype(BF16).reshape(8, 8, LAST)
    for d in (4, 3, 5, 2, 6, 1, 7):
        go("za", "za", za.at[lax.rem(z + d, 8)], zar.at[d - 1], z_of[d])
    total = zb[z].astype(F32)
    got("zb", zbr)
    for d in (1, 7, 2, 6, 3, 5, 4):
        total += zbr[d - 1].astype(F32)
    yb[...] = dot(spread[0:32, 0:24], total.astype(BF16), 1, 0).astype(BF16).reshape(4, 8, WIDE)
    for d in (2, 1, 3):
        go("yb", "yb", yb.at[lax.rem(yl + d, 4)], ybr.at[d - 1], y_of[d])

    got("near", rr.at[1])
    left("slabs", xb.at[0:2])
    left("rest", xb.at[:, 0, 0])
    left("slices", xs.at[:, 0:3])
    left("dx", dx.at[1:4, 0:GROUP])
    left("grads", db)
    got("away", far_r)
    for h in range(2):
        cols = slice(TILE * h, TILE * (h + 1))
        gin_ref[:, cols] = g_ref[:, cols] + (rf[3, h] + rr[1, h].astype(F32) + far_r[h].astype(F32))
    total = yb[yl].astype(F32)
    got("yb", ybr)
    for d in (1, 3, 2):
        total += ybr[d - 1].astype(F32)
    total = total * scale
    for t in range(2):
        gw_ref[t] = total[0:6, GROUP * t : GROUP * (t + 1)]
    total = za[z].astype(F32)
    got("za", zar)
    for d in (1, 7, 2, 6, 3, 5, 4):
        total += zar[d - 1].astype(F32)
    gw_ref[2] = total[0:6, 0:GROUP] * scale

    left("sums", rr)
    left("ya", yar)
    left("yb", ybr)
    left("za", zar)
    left("zb", zbr)


def leave(*refs):
    held, left, done = refs[:3], refs[3:6], refs[6]
    copies = [pltpu.make_async_copy(a, b, done.at[i]) for i, (a, b) in enumerate(zip(held, left))]
    for one in copies:
        one.start()
    for one in copies:
        one.wait()


def shards(inputs, weight, grad_out):
    scale = (inputs.shape[1] * lax.axis_size("seq")) ** (-0.5)
    vmem, hbm = pl.BlockSpec(memory_space=pltpu.VMEM), pl.BlockSpec(memory_space=pltpu.HBM)
    shapes = (
        jax.ShapeDtypeStruct((GROUP, COLS), F32),
        jax.ShapeDtypeStruct((GROUP, COLS), F32),
        jax.ShapeDtypeStruct((3, 6, GROUP), F32),
    )

    def body(*refs):
        kernel(scale, *refs)

    held = pl.pallas_call(
        body,
        out_shape=shapes,
        in_specs=[hbm] * 3,
        out_specs=(vmem,) * 3,
        scratch_shapes=[
            pltpu.VMEM((GROUP, COLS), F32),
            pltpu.VMEM((3, GROUP, 768), BF16),
            pltpu.VMEM((GROUP, COLS), F32),
            pltpu.VMEM((3, 2, 2, GROUP, COLS), BF16),
            pltpu.VMEM((3, 4, 2, 2, 48, COLS), BF16),
            pltpu.VMEM((3, GROUP, 768), BF16),
            pltpu.VMEM((3, 4, GROUP, GROUP), BF16),
            pltpu.VMEM((3, 2, GROUP, TILE), BF16),
            pltpu.VMEM((4, COLS, COLS), BF16),
            pltpu.VMEM((4, COLS, COLS), BF16),
            pltpu.VMEM((4, 48, LAST), BF16),
            pltpu.VMEM((3, 48, LAST), BF16),
            pltpu.VMEM((8, 8, LAST), BF16),
            pltpu.VMEM((7, 8, LAST), BF16),
            pltpu.VMEM((8, 24, WIDE), BF16),
            pltpu.VMEM((7, 24, WIDE), BF16),
            pltpu.VMEM((4, 8, WIDE), BF16),
            pltpu.VMEM((3, 8, WIDE), BF16),
            pltpu.VMEM((4, 2, GROUP, TILE), F32),
            pltpu.VMEM((2, 2, GROUP, TILE), BF16),
            pltpu.VMEM((2, 2, GROUP, TILE), BF16),
            pltpu.VMEM((2, GROUP, TILE), BF16),
            pltpu.VMEM((2, GROUP, TILE), BF16),
            pltpu.SemaphoreType.DMA((3,)),
            pltpu.SemaphoreType.DMA((len(DEPARTURES),)),
            pltpu.SemaphoreType.DMA((len(ARRIVALS),)),
        ],
        compiler_params=pltpu.CompilerParams(collective_id=0, has_side_effects=True, vmem_limit_bytes=20 * 2**20),
    )(*(pltpu.with_memory_space_constraint(a, pltpu.HBM) for a in (inputs, weight, grad_out)))
    return pl.pallas_call(
        leave,
        out_shape=shapes,
        in_specs=[vmem] * 3,
        out_specs=(hbm,) * 3,
        scratch_shapes=[pltpu.SemaphoreType.DMA((3,))],
        compiler_params=pltpu.CompilerParams(vmem_limit_bytes=4 * 2**20),
    )(*held)


def solution(mesh):
    return jax.shard_map(
        shards,
        mesh=mesh,
        in_specs=(P("ch", "seq"), P(None, "ch", None), P("ch", "seq")),
        out_specs=(P("ch", "seq"), P("ch", "seq"), P(None, "seq", "ch")),
        check_vma=False,
    )
```
